256 devices in a mesh: tm: 4 (over x), pix: 64 (over y, z, core).
Axes of the slice: x: 4, y: 4, z: 8, core: 2. Of those that a mesh axis runs over, the one named last changes fastest.
Arguments:
- latent: float32 [16, 256, 448], P(None, 'pix'), may hold values from -6 to 6
- step_size: float32 [8], P('tm'), may hold values from 0.05 to 0.2
- time_embed: float32 [8, 128], P('tm'), may hold values from -6 to 6
- conv_in: bfloat16 [3, 3, 128, 16], replicated, may hold values from -0.5 to 0.5
- conv_mid: bfloat16 [3, 3, 128, 128], replicated, may hold values from -0.1875 to 0.1875
- conv_out: bfloat16 [3, 3, 16, 128], replicated, may hold values from -0.1875 to 0.1875
Outputs:
- trajectory: float32 [8, 16, 256, 448], P('tm', None, 'pix')
The draws below stay inside these ranges and needn't reach their ends.
All inputs are finite; a program needn't handle non-finite values.
Results may differ from the reference program's by a relative error of at most 0.00075.
Values may be sent and summed in bfloat16 or wider, within the bound.
No kernel may reach another device: no remote copies, remote signals or barrier semaphores. Data moves between devices by JAX's collectives and lax.ppermute only.
A program may use at most 64 MiB of HBM per device.

```python
import math
import jax
import jax.numpy as jnp
from jax import lax

C = 16
F = 128
W = 448
ITERS = 3
H = 256
TIMES = 8


def level_of(stream_key, extent, split, low, top_value):
    factor_of, own = 1.0, jax.random.fold_in(stream_key, 6)
    for dim, shards_of in split:
        draws = jnp.exp(jax.random.uniform(jax.random.fold_in(own, dim), (shards_of,), jnp.float32, low / len(split), top_value / len(split)))
        factor_of = factor_of * jnp.repeat(draws, extent[dim] // shards_of).reshape([-1 if axis == dim else 1 for axis in range(len(extent))])
    return factor_of


def scatter_about(rng, shape, deviation, limit, shards=(), kind=jnp.bfloat16):
    gain = level_of(rng, shape, shards, -0.22, 0.18) if shards else 1.0
    entries = jax.random.normal(rng, shape, jnp.float32) * deviation * gain
    return jnp.minimum(jnp.maximum(entries, -limit), limit).astype(kind)


def setup_inputs(seed: int = 0) -> dict:
    arg_keys = jax.random.split(jax.random.key(seed), 7)
    latent = scatter_about(arg_keys[0], (C, H, W), 1.0, 6.0, ((1, 64),), jnp.float32)
    step_size = jnp.clip(jnp.exp(math.log(0.2) - 1.3862944 * jax.random.uniform(arg_keys[1], (TIMES,), jnp.float32) ** level_of(arg_keys[1], (TIMES,), ((0, 4),), -0.2, 0.2)), 0.05, 0.2)
    time_embed = scatter_about(arg_keys[2], (TIMES, F), 1.0, 6.0, ((0, 4),), jnp.float32)
    conv_in = scatter_about(arg_keys[3], (3, 3, F, C), (9 * C) ** -0.5, 0.5)
    conv_mid = scatter_about(arg_keys[4], (3, 3, F, F), (9 * F) ** -0.5, 0.1875)
    conv_out = scatter_about(arg_keys[5], (3, 3, C, F), (9 * F) ** -0.5, 0.1875)
    return {"latent": latent, "step_size": step_size, "time_embed": time_embed, "conv_in": conv_in, "conv_mid": conv_mid, "conv_out": conv_out}


def convolve(values, kernel):
    height = values.shape[1]
    span_cols = values.shape[2]
    padded = jnp.pad(values.astype(jnp.float32), ((0, 0), (1, 1), (1, 1)))
    summed = jnp.zeros((kernel.shape[2], height, span_cols), jnp.float32)
    for row_shift in range(3):
        for col_shift in range(3):
            summed = summed + jnp.einsum("oi,ihw->ohw", kernel[row_shift, col_shift].astype(jnp.float32), padded[:, row_shift:row_shift + height, col_shift:col_shift + span_cols])
    return summed


def reference(latent, step_size, time_embed, conv_in, conv_mid, conv_out):
    def denoise(inputs):
        current, time_vec = inputs
        first_pre = convolve(current.astype(jnp.bfloat16), conv_in) + time_vec[:, None, None]
        hidden = jax.nn.silu(first_pre).astype(jnp.bfloat16)
        second = jax.nn.silu(convolve(hidden, conv_mid)).astype(jnp.bfloat16)
        return current + convolve(second, conv_out)

    states = jnp.broadcast_to(latent[None], (TIMES,) + latent.shape)
    trajectory = states
    for rounds in range(ITERS):
        outputs = lax.map(denoise, (states, time_embed))
        drifts = step_size[:, None, None, None] * outputs
        trajectory = latent[None] + jnp.cumsum(drifts, axis=0)
        states = jnp.concatenate([latent[None], trajectory[:-1]], axis=0)
    return trajectory
```

```python
import functools

import jax
import jax.numpy as jnp
from jax import lax
from jax.experimental import pallas as pl
from jax.experimental.pallas import tpu as pltpu
from jax.sharding import PartitionSpec as P

TIMES = 8
C = 16
F = 128
L = 128
WIN = 22
STARTS = (0, 105, 215, 320)
CUTS = (114, 224, 334)
BF = jnp.bfloat16
F32 = jnp.float32

ROUNDS = ((0, 1, 10), (1, 4, 7), (2, 7, 4))


def shift_cols(x, by):
    lane = lax.broadcasted_iota(jnp.int32, x.shape, x.ndim - 1)
    moved = pltpu.roll(x, by % L, x.ndim - 1)
    return jnp.where(lane == (0 if by == 1 else L - 1), jnp.zeros_like(x), moved)


def body(place, step, lat, win2, conv_mid, conv_out, out, st_a, st_b, low, hid, sec, acc, w_mid, w_out):
    base, tm = place[0], place[1]
    edge = (base < 0) | (base + WIN > 256)

    w_mid[...] = jnp.zeros_like(w_mid)
    w_out[...] = jnp.zeros_like(w_out)
    for a in range(3):
        for b in range(3):
            mid = conv_mid[a, b] * 0.5
            tail = conv_out[a, b]
            for q in range(2):
                w_mid[q * F:(q + 1) * F, ((a + q) * 3 + b) * F:((a + q) * 3 + b + 1) * F] = mid
                w_out[q * 48 + b * C:q * 48 + (b + 1) * C, (a + q) * F:(a + q + 1) * F] = tail

    def clear_outside(ref, rows, size):
        @pl.when(edge)
        def _():
            def one(w, _):
                @pl.when((base + w < 0) | (base + w >= 256))
                def _():
                    ref[pl.ds(pl.multiple_of(w * size, size), size), :] = jnp.zeros((size, ref.shape[1]), ref.dtype)
                return 0
            lax.fori_loop(rows[0], rows[1], one, 0)

    def load_rows(w, _):
        x = lat[w]
        for j in range(TIMES):
            st_a[j, w] = x
        return 0

    lax.fori_loop(0, WIN, load_rows, 0)

    states, following = st_a, st_b
    for rounds, (first, h0, pairs) in enumerate(ROUNDS):
        groups = []
        t = first
        while t < TIMES:
            groups.append((t, min(4, TIMES - t)))
            t += 4
        for t0, n in groups:
            width = n * L

            def fill(w, _, t0=t0, n=n, states=states):
                for i in range(n):
                    x = states[t0 + i, w]
                    both = jnp.concatenate([shift_cols(x, 1), x, shift_cols(x, -1)], axis=0).astype(BF)
                    low[pl.ds(pl.multiple_of(w * 48, 48), 48), i * L:(i + 1) * L] = both
                return 0

            lax.fori_loop(h0 - 1, h0 + 2 * pairs + 1, fill, 0)
            clear_outside(low, (h0 - 1, h0 + 2 * pairs + 1), 48)

            r = lax.broadcasted_iota(jnp.int32, (64, width), 0)
            c = lax.broadcasted_iota(jnp.int32, (64, width), 1)
            pick = jnp.where(((r & 7) == t0 + (c >> 7)) & (r < 24), 1.0, 0.0).astype(BF)

            def hidden_pair(p, _, n=n, width=width, h0=h0, pick=pick):
                h = h0 + 2 * p
                rhs = jnp.concatenate([low[pl.ds(pl.multiple_of((h - 1) * 48, 48), 192), :width], pick], axis=0)
                v = jnp.dot(win2[...], rhs, preferred_element_type=F32)
                v = v + v * jnp.tanh(v)
                for q in range(2):
                    for i in range(n):
                        x = v[q * F:(q + 1) * F, i * L:(i + 1) * L]
                        at = pl.multiple_of((h + q) * 384, 384)
                        hid[pl.ds(at, F), i * L:(i + 1) * L] = shift_cols(x, 1).astype(BF)
                        hid[pl.ds(at + F, F), i * L:(i + 1) * L] = x.astype(BF)
                        hid[pl.ds(at + 2 * F, F), i * L:(i + 1) * L] = shift_cols(x, -1).astype(BF)
                return 0

            lax.fori_loop(0, pairs, hidden_pair, 0)
            clear_outside(hid, (h0, h0 + 2 * pairs), 384)

            def second_pair(p, _, width=width, h0=h0):
                s = h0 + 1 + 2 * p
                v = jnp.dot(w_mid[...], hid[pl.ds(pl.multiple_of((s - 1) * 384, 384), 1536), :width], preferred_element_type=F32)
                v = v + v * jnp.tanh(v)
                sec[pl.ds(pl.multiple_of(s * F, F), 2 * F), :width] = v.astype(BF)
                return 0

            lax.fori_loop(0, pairs - 1, second_pair, 0)
            clear_outside(sec, (h0 + 1, h0 + 2 * pairs - 1), F)

            def out_pair(p, _, t0=t0, n=n, width=width, h0=h0, first=first, rounds=rounds, states=states, following=following):
                r0 = h0 + 2 + 2 * p
                y = jnp.dot(w_out[...], sec[pl.ds(pl.multiple_of((r0 - 1) * F, F), 4 * F), :width], preferred_element_type=F32)
                for q in range(2):
                    row = r0 + q
                    x = lat[row]
                    if t0 == 0:
                        total = jnp.zeros((C, L), F32)
                    else:
                        total = acc[row]
                    for i in range(n):
                        t = t0 + i
                        part = y[q * 48:(q + 1) * 48, i * L:(i + 1) * L]
                        new = states[t, row] + (shift_cols(part[:C], 1) + part[C:2 * C] + shift_cols(part[2 * C:], -1))
                        total = total + step[t] * new
                        if rounds == 2:
                            out[(t // 2) ^ tm, t % 2, row - 9] = x + total
                        elif t + 1 < TIMES:
                            following[t + 1, row] = x + total
                        if t == rounds and rounds < 2:
                            kept_at = acc
                            kept_at[WIN + row] = total
                            if rounds + 1 == 2 or rounds == 0:
                                @pl.when((row >= 9) & (row < 13))
                                def _(t=t, row=row, value=x + total):
                                    out[(t // 2) ^ tm, t % 2, row - 9] = value
                    acc[row] = total
                return 0

            if t0 == first and first > 0:
                def restore(w, _):
                    acc[w] = acc[WIN + w]
                    return 0
                lax.fori_loop(0, WIN, restore, 0)
            lax.fori_loop(0, pairs - 2, out_pair, 0)
        states, following = following, states


def main_kernel(place, step, lat, win2, conv_mid, conv_out):
    vm = pl.BlockSpec(memory_space=pltpu.VMEM)
    sm = pl.BlockSpec(memory_space=pltpu.SMEM)
    return pl.pallas_call(
        body,
        out_shape=jax.ShapeDtypeStruct((4, 2, 4, C, L), F32),
        in_specs=[sm, sm, vm, vm, vm, vm],
        out_specs=vm,
        scratch_shapes=[
            pltpu.VMEM((TIMES, WIN, C, L), F32),
            pltpu.VMEM((TIMES, WIN, C, L), F32),
            pltpu.VMEM((WIN * 48, 4 * L), BF),
            pltpu.VMEM((WIN * 384, 4 * L), BF),
            pltpu.VMEM((WIN * F, 4 * L), BF),
            pltpu.VMEM((2 * WIN, C, L), F32),
            pltpu.VMEM((2 * F, 12 * F), BF),
            pltpu.VMEM((96, 4 * F), BF),
        ],
        compiler_params=pltpu.CompilerParams(vmem_limit_bytes=48 << 20),
        name="picard",
    )(place, step, lat, win2, conv_mid, conv_out)


def join_body(place, p0, p1, p2, p3, out):
    tm = place[1]
    pieces = [p0[...], p1[...], p2[...], p3[...]]
    lane = lax.broadcasted_iota(jnp.int32, pieces[0].shape, 1)
    placed = []
    for t in range(4):
        k = t ^ tm
        x = jnp.where(k == 0, pieces[0], jnp.where(k == 1, pieces[1], jnp.where(k == 2, pieces[2], pieces[3])))
        placed.append(pltpu.roll(x, STARTS[t] % L, 1) if STARTS[t] % L else x)
    for g in range(3):
        out[:, g * L:(g + 1) * L] = jnp.where(lane < CUTS[g] - g * L, placed[g], placed[g + 1])
    out[:, 3 * L:] = placed[3][:, :448 - 3 * L]


def join(place, pieces):
    vm = pl.BlockSpec(memory_space=pltpu.VMEM)
    return pl.pallas_call(
        join_body,
        out_shape=jax.ShapeDtypeStruct((128, 448), F32),
        in_specs=[pl.BlockSpec(memory_space=pltpu.SMEM)] + [vm] * 4,
        out_specs=vm,
        name="join",
    )(place, *pieces)


def across(x, k):
    return lax.ppermute(x, "tm", [(t, t ^ k) for t in range(4)])


def pair_up(x, pairs):
    return lax.ppermute(x, "pix", [(a, b) for a, b in pairs] + [(b, a) for a, b in pairs])


CORES = [(2 * k, 2 * k + 1) for k in range(32)]
CHIPS = [(2 * k + 1, 2 * k + 2) for k in range(31)]
FAR = [(2 * k + 1, 2 * k + 4) for k in range(30)]


def gather_rows(own, core):
    edge_row = jnp.where(core == 0, own[:1], own[3:])
    far = pair_up(edge_row, FAR)
    partner = pair_up(own, CORES)
    chip = jnp.where(core == 0, jnp.concatenate([own, partner]), jnp.concatenate([partner, own]))
    near = pair_up(chip, CHIPS)
    other = pair_up(jnp.where(core == 0, near[3:], near[:5]), CORES)
    return jnp.where(core == 0, jnp.concatenate([far, near, chip, other]), jnp.concatenate([other, chip, near, far]))


def shards(latent, step_size, time_embed, conv_in, conv_mid, conv_out):
    tm, pix = lax.axis_index("tm"), lax.axis_index("pix")
    start = jnp.where(tm == 0, STARTS[0], jnp.where(tm == 1, STARTS[1], jnp.where(tm == 2, STARTS[2], STARTS[3])))
    own = lax.dynamic_slice(latent, (0, 0, start), (C, 4, L)).transpose(1, 0, 2)
    place = jnp.stack([4 * pix - 9, tm]).astype(jnp.int32)

    small = jnp.concatenate([time_embed, jnp.broadcast_to(step_size[:, None], (2, F))])
    parts = jnp.stack([small] + [across(small, k) for k in (1, 2, 3)])
    every = jnp.concatenate([lax.dynamic_index_in_dim(parts, t ^ tm, 0, keepdims=False)[None] for t in range(4)])
    embed = every[:, :2].reshape(TIMES, F) * 0.5
    step = every[:, 2:, 0].reshape(TIMES)

    lat = gather_rows(own, pix % 2)

    hi = lax.reduce_precision(embed, 8, 7)
    rest = embed - hi
    mid = lax.reduce_precision(rest, 8, 7)
    te = jnp.concatenate([hi, mid, rest - mid]).T.astype(BF)
    flat = (conv_in * 0.5).transpose(2, 0, 1, 3).reshape(F, 144)
    wide = jnp.concatenate([jnp.pad(flat, ((0, 0), (0, 48))), jnp.pad(flat, ((0, 0), (48, 0)))])
    win2 = jnp.concatenate([wide, jnp.pad(jnp.concatenate([te, te]), ((0, 0), (0, 40)))], axis=1)

    pieces = main_kernel(place, step, lat, win2, conv_mid, conv_out).reshape(4, 128, L)
    got = [pieces[0]] + [across(pieces[k], k) for k in (1, 2, 3)]
    return join(place, got).reshape(2, 4, C, 448).transpose(0, 2, 1, 3)


def solution(mesh):
    in_specs = (P(None, "pix", None), P("tm"), P("tm", None), P(), P(), P())
    out_specs = P("tm", None, "pix", None)
    return jax.shard_map(shards, mesh=mesh, in_specs=in_specs, out_specs=out_specs, check_vma=False)
```

```python
import functools

import jax
import jax.numpy as jnp
from jax import lax
from jax.experimental import pallas as pl
from jax.experimental.pallas import tpu as pltpu
from jax.sharding import PartitionSpec as P

TIMES = 8
C = 16
F = 128
L = 128
ROWS = 4
STARTS = (-1, 105, 215, 321)
CUTS = (114, 224, 334)
BF = jnp.bfloat16
F32 = jnp.float32


def prepare_body(conv_mid, conv_out, w_mid, w_out):
    w_mid[...] = jnp.zeros_like(w_mid)
    w_out[...] = jnp.zeros_like(w_out)
    for a in range(3):
        for b in range(3):
            mid = conv_mid[a, b] * 0.5
            tail = conv_out[a, b]
            for q in range(2):
                w_mid[q * F:(q + 1) * F, ((a + q) * 3 + b) * F:((a + q) * 3 + b + 1) * F] = mid
                w_out[q * 48 + b * C:q * 48 + (b + 1) * C, (a + q) * F:(a + q + 1) * F] = tail


VM = pl.BlockSpec(memory_space=pltpu.VMEM)
SM = pl.BlockSpec(memory_space=pltpu.SMEM)


def prepare(conv_mid, conv_out):
    return pl.pallas_call(
        prepare_body,
        out_shape=(jax.ShapeDtypeStruct((3 * F, 12 * F), BF), jax.ShapeDtypeStruct((96, 4 * F), BF)),
        in_specs=[VM, VM],
        out_specs=(VM, VM),
        name="prepare",
    )(conv_mid, conv_out)


def silu2(v):
    return v + v * jnp.tanh(v)


def round_body(rounds, place, step, lat, prior, from_a, from_b, w_in, w_mid, w_out, *rest):
    pix, tm = place[0], place[1]
    core = pix % 2
    last = rounds == 2
    if last:
        out, *rest = rest
        low, hid, sec = rest[:2], rest[2:10], rest[10:16]
    else:
        nxt, to_a, to_b, *rest = rest
        low, hid, sec = rest[:2], rest[2:10], rest[10:16]
    groups = [(t0, min(4, TIMES - t0)) for t0 in (rounds, rounds + 4)]

    lane = lax.broadcasted_iota(jnp.int32, (C, L), 1)
    column = jnp.where(((tm == 0) & (lane == 0)) | ((tm == 3) & (lane == L - 1)), 0.0, 1.0)

    def state(t, row):
        return lat[row] if rounds == 0 else prior[t, row]

    def spread(x):
        x = x * column
        return jnp.concatenate([pltpu.roll(x, 1, 1) * column, x, pltpu.roll(x, L - 1, 1) * column], axis=0).astype(BF)

    def fill(g):
        t0, n = groups[g]
        for w in range(10):
            for i in range(n if rounds else 1):
                if 3 <= w < 7:
                    x = state(t0 + i, w - 3)
                else:
                    d = w if w < 3 else w - 7
                    at = (t0 + i - rounds, d) if rounds else (d,)
                    a, b = from_a[at].astype(F32), from_b[at].astype(F32)
                    x = jnp.where((core == 0) == (w < 3), b, a)
                x = spread(x)
                for lanes in ([i] if rounds else range(n)):
                    low[g][w * 48:(w + 1) * 48, lanes * L:(lanes + 1) * L] = x

    def weights(ref, top_inside, bottom_inside):
        top = 0 if top_inside is None else pl.multiple_of(jnp.where(top_inside, 0, 2 * F), F)
        bottom = F if bottom_inside is None else pl.multiple_of(jnp.where(bottom_inside, F, 2 * F), F)
        return jnp.concatenate([ref[pl.ds(top, F), :], ref[pl.ds(bottom, F), :]], axis=0)

    above, below = pix > 0, pix < 63

    def hidden_pair(g, p):
        t0, n = groups[g]
        width = n * L
        r = lax.broadcasted_iota(jnp.int32, (64, width), 0)
        c = lax.broadcasted_iota(jnp.int32, (64, width), 1)
        edge = ((tm == 0) & ((c & 127) == 0)) | ((tm == 3) & ((c & 127) == L - 1))
        pick = jnp.where(((r & 7) == t0 + (c >> 7)) & (r < 24) & jnp.logical_not(edge), 1.0, 0.0).astype(BF)
        rhs = jnp.concatenate([low[g][2 * p * 48:2 * p * 48 + 192, :width], pick], axis=0)
        inside = above if p == 0 else below if p == 3 else None
        v = silu2(jnp.dot(weights(w_in, inside, inside), rhs, preferred_element_type=F32))
        to = hid[g * 4 + p]
        for i in range(n):
            for q in range(2):
                x = v[q * F:(q + 1) * F, i * L:(i + 1) * L]
                at = q * 384
                to[at:at + F, i * L:(i + 1) * L] = pltpu.roll(x, 1, 1).astype(BF)
                to[at + F:at + 2 * F, i * L:(i + 1) * L] = x.astype(BF)
                to[at + 2 * F:at + 3 * F, i * L:(i + 1) * L] = pltpu.roll(x, L - 1, 1).astype(BF)

    def second_pair(g, p):
        width = groups[g][1] * L
        rhs = jnp.concatenate([hid[g * 4 + p][:, :width], hid[g * 4 + p + 1][:, :width]], axis=0)
        w = weights(w_mid, above if p == 0 else None, below if p == 2 else None)
        sec[g * 3 + p][:, :width] = silu2(jnp.dot(w, rhs, preferred_element_type=F32)).astype(BF)

    totals = [jnp.zeros((C, L), F32) if rounds == 0 else prior[0, row] for row in range(ROWS)]

    def out_pair(g, p):
        t0, n = groups[g]
        width = n * L
        rhs = jnp.concatenate([sec[g * 3 + p][:, :width], sec[g * 3 + p + 1][:, :width]], axis=0)
        y = jnp.dot(w_out[...], rhs, preferred_element_type=F32)
        for q in range(2):
            row = 2 * p + q
            for i in range(n):
                t = t0 + i
                part = y[q * 48:(q + 1) * 48, i * L:(i + 1) * L]
                conv = pltpu.roll(part[:C] * column, 1, 1) + part[C:2 * C] + pltpu.roll(part[2 * C:] * column, L - 1, 1)
                totals[row] = totals[row] + step[t] * (state(t, row) + conv)
                value = lat[row] + totals[row]
                if last:
                    out[(t // 2) ^ tm, t % 2, row] = value
                else:
                    nxt[t + 1, row] = value
                    if t == rounds:
                        nxt[0, row] = totals[row]

    fill(0)
    for p in range(4):
        hidden_pair(0, p)
    fill(1)
    second_pair(0, 0)
    hidden_pair(1, 0)
    second_pair(0, 1)
    hidden_pair(1, 1)
    second_pair(0, 2)
    hidden_pair(1, 2)
    out_pair(0, 0)
    hidden_pair(1, 3)
    out_pair(0, 1)
    for p in range(3):
        second_pair(1, p)
    for p in range(2):
        out_pair(1, p)

    for row in range(ROWS):
        if rounds == 1:
            nxt[1, row] = prior[1, row]
        if last:
            for t in range(2):
                out[(t // 2) ^ tm, t % 2, row] = prior[t + 1, row]
    if not last:
        for t in range(rounds + 1, TIMES):
            for d in range(3):
                to_a[t - rounds - 1, d] = nxt[t, d + 1 - core].astype(BF)
                to_b[t - rounds - 1, d] = nxt[t, d + core].astype(BF)


def run_round(rounds, place, step, lat, prior, from_a, from_b, w_in, w_mid, w_out):
    if rounds == 2:
        out_shape = jax.ShapeDtypeStruct((4, 2, ROWS, C, L), F32)
        out_specs = VM
    else:
        sent = jax.ShapeDtypeStruct((TIMES - 1 - rounds, 3, C, L), BF)
        out_shape = (jax.ShapeDtypeStruct((TIMES + 1, ROWS, C, L), F32), sent, sent)
        out_specs = (VM, VM, VM)
    return pl.pallas_call(
        functools.partial(round_body, rounds),
        out_shape=out_shape,
        in_specs=[SM, SM] + [VM] * 7,
        out_specs=out_specs,
        scratch_shapes=[pltpu.VMEM((480, 4 * L), BF)] * 2 + [pltpu.VMEM((768, 4 * L), BF)] * 8 + [pltpu.VMEM((2 * F, 4 * L), BF)] * 6,
        compiler_params=pltpu.CompilerParams(vmem_limit_bytes=40 << 20),
        name="round%d" % rounds,
    )(place, step, lat, prior, from_a, from_b, w_in, w_mid, w_out)


def join_body(place, p0, p1, p2, p3, out):
    tm = place[1]
    pieces = [p0[...], p1[...], p2[...], p3[...]]
    lane = lax.broadcasted_iota(jnp.int32, pieces[0].shape, 1)
    placed = []
    for t in range(4):
        k = t ^ tm
        x = jnp.where(k == 0, pieces[0], jnp.where(k == 1, pieces[1], jnp.where(k == 2, pieces[2], pieces[3])))
        placed.append(pltpu.roll(x, STARTS[t] % L, 1) if STARTS[t] % L else x)
    for g in range(3):
        out[:, g * L:(g + 1) * L] = jnp.where(lane < CUTS[g] - g * L, placed[g], placed[g + 1])
    out[:, 3 * L:] = placed[3][:, :448 - 3 * L]


def join(place, pieces):
    return pl.pallas_call(
        join_body,
        out_shape=jax.ShapeDtypeStruct((128, 448), F32),
        in_specs=[SM] + [VM] * 4,
        out_specs=VM,
        name="join",
    )(place, *pieces)


def across(x, k):
    return lax.ppermute(x, "tm", [(t, t ^ k) for t in range(4)])


def pair_up(x, pairs):
    return lax.ppermute(x, "pix", [(a, b) for a, b in pairs] + [(b, a) for a, b in pairs])


CORES = [(2 * k, 2 * k + 1) for k in range(32)]
CHIPS = [(2 * k + 1, 2 * k + 2) for k in range(31)]


def shards(latent, step_size, time_embed, conv_in, conv_mid, conv_out):
    tm, pix = lax.axis_index("tm"), lax.axis_index("pix")
    core = pix % 2
    start = jnp.where(tm == 0, STARTS[0], jnp.where(tm == 1, STARTS[1], jnp.where(tm == 2, STARTS[2], STARTS[3])))
    padded = jnp.pad(latent, ((0, 0), (0, 0), (1, 1)))
    lat = lax.dynamic_slice(padded, (0, 0, start + 1), (C, ROWS, L)).transpose(1, 0, 2)
    place = jnp.stack([pix, tm]).astype(jnp.int32)

    rounded = lat.astype(BF)
    to_a = jnp.where(core == 0, rounded[1:], rounded[:3])
    to_b = jnp.where(core == 0, rounded[:3], rounded[1:])
    from_b, from_a = pair_up(to_b, CHIPS), pair_up(to_a, CORES)

    small = jnp.concatenate([time_embed, jnp.broadcast_to(step_size[:, None], (2, F))])
    parts = jnp.stack([small] + [across(small, k) for k in (1, 2, 3)])
    every = jnp.concatenate([lax.dynamic_index_in_dim(parts, t ^ tm, 0, keepdims=False)[None] for t in range(4)])
    embed = every[:, :2].reshape(TIMES, F) * 0.5
    step = every[:, 2:, 0].reshape(TIMES)

    hi = lax.reduce_precision(embed, 8, 7)
    rest = embed - hi
    mid = lax.reduce_precision(rest, 8, 7)
    te = jnp.concatenate([hi, mid, rest - mid]).T.astype(BF)
    flat = (conv_in * 0.5).transpose(2, 0, 1, 3).reshape(F, 144)
    wide = jnp.concatenate([jnp.pad(flat, ((0, 0), (0, 48))), jnp.pad(flat, ((0, 0), (48, 0)))])
    w_in = jnp.concatenate([wide, jnp.pad(jnp.concatenate([te, te]), ((0, 0), (0, 40)))], axis=1)
    w_in = jnp.pad(w_in, ((0, F), (0, 0)))
    w_mid, w_out = prepare(conv_mid, conv_out)

    prior = lat
    for rounds in range(2):
        prior, to_a, to_b = run_round(rounds, place, step, lat, prior, from_a, from_b, w_in, w_mid, w_out)
        from_b, from_a = pair_up(to_b, CHIPS), pair_up(to_a, CORES)
    pieces = run_round(2, place, step, lat, prior, from_a, from_b, w_in, w_mid, w_out).reshape(4, 128, L)
    got = [pieces[0]] + [across(pieces[k], k) for k in (1, 2, 3)]
    return join(place, got).reshape(2, 4, C, 448).transpose(0, 2, 1, 3)


def solution(mesh):
    in_specs = (P(None, "pix", None), P("tm"), P("tm", None), P(), P(), P())
    out_specs = P("tm", None, "pix", None)
    return jax.shard_map(shards, mesh=mesh, in_specs=in_specs, out_specs=out_specs, check_vma=False)
```

```python
import functools

import jax
import jax.numpy as jnp
from jax import lax
from jax.experimental import pallas as pl
from jax.experimental.pallas import tpu as pltpu
from jax.sharding import PartitionSpec as P

TIMES = 8
C = 16
F = 128
L = 128
ROWS = 4
STARTS = (-1, 105, 215, 321)
SHIFTS = tuple(-start % L for start in STARTS)
CUTS = (114, 224, 334)
BF = jnp.bfloat16
F32 = jnp.float32


VM = pl.BlockSpec(memory_space=pltpu.VMEM)
SM = pl.BlockSpec(memory_space=pltpu.SMEM)


def by_tm(tm, values):
    return jnp.where(tm == 0, values[0], jnp.where(tm == 1, values[1], jnp.where(tm == 2, values[2], values[3])))


def enter_body(step, latent, embed, lat, to_a, to_b, small):
    tm, core = lax.axis_index("tm"), lax.axis_index("pix") % 2
    shift = by_tm(tm, SHIFTS)
    lane = lax.broadcasted_iota(jnp.int32, (C, L), 1)
    for r in range(ROWS):
        tiles = [jnp.zeros((C, L), F32)] + [latent[:, r, g * L:(g + 1) * L] for g in range(3)]
        tiles.append(jnp.concatenate([latent[:, r, 3 * L:], jnp.zeros((C, 4 * L - 448), F32)], axis=1))
        left, right = by_tm(tm, tiles[:4]), by_tm(tm, tiles[1:])
        lat[r] = jnp.where(lane < shift, pltpu.roll(left, shift, 1), pltpu.roll(right, shift, 1))
    for d in range(3):
        to_a[d] = lat[d + 1 - core].astype(BF)
        to_b[d] = lat[d + core].astype(BF)
    small[0:2] = embed[...]
    for d in range(2):
        small[2 + d:3 + d] = jnp.full((1, F), step[d], F32)


def enter(step, latent, embed):
    sent = jax.ShapeDtypeStruct((3, C, L), BF)
    return pl.pallas_call(
        enter_body,
        out_shape=(jax.ShapeDtypeStruct((ROWS, C, L), F32), sent, sent, jax.ShapeDtypeStruct((4, F), F32)),
        in_specs=[SM, VM, VM],
        out_specs=(VM,) * 4,
        compiler_params=pltpu.CompilerParams(vmem_limit_bytes=4 << 20),
        name="enter",
    )(step, latent, embed)


def prepare(tm, smalls, conv_in, conv_mid, conv_out, w_in, w_mid, w_out, steps, gathered, turned):
    w_mid[...] = jnp.zeros_like(w_mid)
    w_out[...] = jnp.zeros_like(w_out)
    turned[...] = jnp.zeros_like(turned)
    for a in range(3):
        for b in range(3):
            mid = conv_mid[a, b] * 0.5
            tail = conv_out[a, b]
            head = conv_in[a, b] * 0.5
            for q in range(2):
                w_mid[q * F:(q + 1) * F, ((a + q) * 3 + b) * F:((a + q) * 3 + b + 1) * F] = mid
                w_out[q * 48 + b * C:q * 48 + (b + 1) * C, (a + q) * F:(a + q + 1) * F] = tail
                turned[(a + q) * 48 + b * C:(a + q) * 48 + (b + 1) * C, q * F:(q + 1) * F] = head
    for k in range(4):
        gathered[tm ^ k] = smalls[k][...]
    embed = jnp.concatenate([gathered[t, 0:2] for t in range(4)], axis=0) * 0.5
    steps[...] = jnp.concatenate([gathered[t, 2:4] for t in range(4)], axis=0)
    high = embed.astype(BF).astype(F32)
    rest = embed - high
    middle = rest.astype(BF).astype(F32)
    tail = jnp.concatenate([high, middle, rest - middle, jnp.zeros((40, F), F32)], axis=0).astype(BF)
    for q in range(2):
        turned[192:, q * F:(q + 1) * F] = tail
    w_in[:2 * F] = turned[...].astype(F32).T.astype(BF)
    w_in[2 * F:] = jnp.zeros((F, 2 * F), BF)


def silu2(v):
    return v + v * jnp.tanh(v)


def round_body(rounds, *refs):
    pix, tm = lax.axis_index("pix"), lax.axis_index("tm")
    core = pix % 2
    last = rounds == 2
    if rounds == 0:
        lat, from_a, from_b, *smalls = refs[:7]
        conv_in, conv_mid, conv_out, nxt, to_a, to_b, w_in, w_mid, w_out, steps, *rest = refs[7:]
        prior = None
        prepare(tm, smalls, conv_in, conv_mid, conv_out, w_in, w_mid, w_out, steps, *rest[16:])
    else:
        lat, from_a, from_b, prior, w_in, w_mid, w_out, steps = refs[:8]
        if last:
            out, rest, ready = refs[8:12], refs[12:], refs[-1]
        else:
            nxt, to_a, to_b, *rest = refs[8:]
    low, hid, sec = rest[:2], rest[2:10], rest[10:16]
    groups = [(t0, min(4, TIMES - t0)) for t0 in (rounds, rounds + 4)]

    lane = lax.broadcasted_iota(jnp.int32, (C, L), 1)
    column = jnp.where(((tm == 0) & (lane == 0)) | ((tm == 3) & (lane == L - 1)), 0.0, 1.0)

    def state(t, row):
        return lat[row] if rounds == 0 else prior[t, row]

    def spread(x):
        x = x * column
        return jnp.concatenate([pltpu.roll(x, 1, 1) * column, x, pltpu.roll(x, L - 1, 1) * column], axis=0).astype(BF)

    def fill(g):
        t0, n = groups[g]
        for w in range(10):
            for i in range(n if rounds else 1):
                if 3 <= w < 7:
                    x = state(t0 + i, w - 3)
                else:
                    d = w if w < 3 else w - 7
                    at = (t0 + i - rounds, d) if rounds else (d,)
                    a, b = from_a[at].astype(F32), from_b[at].astype(F32)
                    x = jnp.where((core == 0) == (w < 3), b, a)
                x = spread(x)
                for lanes in ([i] if rounds else range(n)):
                    low[g][w * 48:(w + 1) * 48, lanes * L:(lanes + 1) * L] = x

    def weights(ref, top_inside, bottom_inside):
        top = 0 if top_inside is None else pl.multiple_of(jnp.where(top_inside, 0, 2 * F), F)
        bottom = F if bottom_inside is None else pl.multiple_of(jnp.where(bottom_inside, F, 2 * F), F)
        return jnp.concatenate([ref[pl.ds(top, F), :], ref[pl.ds(bottom, F), :]], axis=0)

    above, below = pix > 0, pix < 63

    def hidden_pair(g, p):
        t0, n = groups[g]
        width = n * L
        r = lax.broadcasted_iota(jnp.int32, (64, width), 0)
        c = lax.broadcasted_iota(jnp.int32, (64, width), 1)
        edge = ((tm == 0) & ((c & 127) == 0)) | ((tm == 3) & ((c & 127) == L - 1))
        pick = jnp.where(((r & 7) == t0 + (c >> 7)) & (r < 24) & jnp.logical_not(edge), 1.0, 0.0).astype(BF)
        rhs = jnp.concatenate([low[g][2 * p * 48:2 * p * 48 + 192, :width], pick], axis=0)
        inside = above if p == 0 else below if p == 3 else None
        v = silu2(jnp.dot(weights(w_in, inside, inside), rhs, preferred_element_type=F32))
        to = hid[g * 4 + p]
        for i in range(n):
            for q in range(2):
                x = v[q * F:(q + 1) * F, i * L:(i + 1) * L]
                at = q * 384
                to[at:at + F, i * L:(i + 1) * L] = pltpu.roll(x, 1, 1).astype(BF)
                to[at + F:at + 2 * F, i * L:(i + 1) * L] = x.astype(BF)
                to[at + 2 * F:at + 3 * F, i * L:(i + 1) * L] = pltpu.roll(x, L - 1, 1).astype(BF)

    def second_pair(g, p):
        width = groups[g][1] * L
        rhs = jnp.concatenate([hid[g * 4 + p][:, :width], hid[g * 4 + p + 1][:, :width]], axis=0)
        w = weights(w_mid, above if p == 0 else None, below if p == 2 else None)
        sec[g * 3 + p][:, :width] = silu2(jnp.dot(w, rhs, preferred_element_type=F32)).astype(BF)

    def keep(t, row, value):
        ready[pl.ds(((t // 2) ^ tm) * 128 + (t % 2) * 64 + row, C, stride=ROWS), :] = value

    totals = [jnp.zeros((C, L), F32) if rounds == 0 else prior[0, row] for row in range(ROWS)]

    def out_pair(g, p):
        t0, n = groups[g]
        width = n * L
        rhs = jnp.concatenate([sec[g * 3 + p][:, :width], sec[g * 3 + p + 1][:, :width]], axis=0)
        y = jnp.dot(w_out[...], rhs, preferred_element_type=F32)
        for q in range(2):
            row = 2 * p + q
            for i in range(n):
                t = t0 + i
                part = y[q * 48:(q + 1) * 48, i * L:(i + 1) * L]
                conv = pltpu.roll(part[:C] * column, 1, 1) + part[C:2 * C] + pltpu.roll(part[2 * C:] * column, L - 1, 1)
                totals[row] = totals[row] + steps[t:t + 1] * (state(t, row) + conv)
                value = lat[row] + totals[row]
                if last:
                    keep(t, row, value)
                else:
                    nxt[t + 1, row] = value
                    if t == rounds:
                        nxt[0, row] = totals[row]

    fill(0)
    for p in range(4):
        hidden_pair(0, p)
    fill(1)
    second_pair(0, 0)
    hidden_pair(1, 0)
    second_pair(0, 1)
    hidden_pair(1, 1)
    second_pair(0, 2)
    hidden_pair(1, 2)
    out_pair(0, 0)
    hidden_pair(1, 3)
    out_pair(0, 1)
    for p in range(3):
        second_pair(1, p)
    for p in range(2):
        out_pair(1, p)

    for row in range(ROWS):
        if rounds == 1:
            nxt[1, row] = prior[1, row]
        if last:
            for t in range(2):
                keep(t, row, prior[t + 1, row])
    if last:
        for k in range(4):
            out[k][...] = ready[k * 128:(k + 1) * 128].reshape(32, ROWS, L)
    else:
        for t in range(rounds + 1, TIMES):
            for d in range(3):
                to_a[t - rounds - 1, d] = nxt[t, d + 1 - core].astype(BF)
                to_b[t - rounds - 1, d] = nxt[t, d + core].astype(BF)


def run_round(rounds, *args):
    scratch = [pltpu.VMEM((480, 4 * L), BF)] * 2 + [pltpu.VMEM((768, 4 * L), BF)] * 8 + [pltpu.VMEM((2 * F, 4 * L), BF)] * 6
    if rounds == 2:
        out_shape = (jax.ShapeDtypeStruct((32, ROWS, L), F32),) * 4
        scratch += [pltpu.VMEM((512, L), F32)]
    else:
        sent = jax.ShapeDtypeStruct((TIMES - 1 - rounds, 3, C, L), BF)
        out_shape = (jax.ShapeDtypeStruct((TIMES + 1, ROWS, C, L), F32), sent, sent)
    if rounds == 0:
        tables = ((3 * F, 2 * F), (3 * F, 12 * F), (96, 4 * F))
        out_shape += tuple(jax.ShapeDtypeStruct(shape, BF) for shape in tables) + (jax.ShapeDtypeStruct((TIMES, F), F32),)
        scratch += [pltpu.VMEM((4, 4, F), F32), pltpu.VMEM((2 * F, 2 * F), BF)]
    return pl.pallas_call(
        functools.partial(round_body, rounds),
        out_shape=out_shape,
        in_specs=[VM] * len(args),
        out_specs=(VM,) * len(out_shape),
        scratch_shapes=scratch,
        compiler_params=pltpu.CompilerParams(vmem_limit_bytes=40 << 20),
        name="round%d" % rounds,
    )(*args)


def join_body(p0, p1, p2, p3, out):
    tm = lax.axis_index("tm")
    pieces = [p0[...], p1[...], p2[...], p3[...]]
    lane = lax.broadcasted_iota(jnp.int32, pieces[0].shape, 2)
    placed = []
    for t in range(4):
        x = by_tm(t ^ tm, pieces)
        placed.append(pltpu.roll(x, STARTS[t] % L, 2))
    for g in range(3):
        out[:, :, g * L:(g + 1) * L] = jnp.where(lane < CUTS[g] - g * L, placed[g], placed[g + 1])
    out[:, :, 3 * L:] = placed[3][:, :, :448 - 3 * L]


def join(pieces):
    return pl.pallas_call(
        join_body,
        out_shape=jax.ShapeDtypeStruct((32, ROWS, 448), F32),
        in_specs=[VM] * 4,
        out_specs=VM,
        compiler_params=pltpu.CompilerParams(vmem_limit_bytes=8 << 20),
        name="join",
    )(*pieces)


def across(x, k):
    return lax.ppermute(x, "tm", [(t, t ^ k) for t in range(4)])


def pair_up(x, pairs):
    return lax.ppermute(x, "pix", [(a, b) for a, b in pairs] + [(b, a) for a, b in pairs])


CORES = [(2 * k, 2 * k + 1) for k in range(32)]
CHIPS = [(2 * k + 1, 2 * k + 2) for k in range(31)]


def shards(latent, step_size, time_embed, conv_in, conv_mid, conv_out):
    lat, to_a, to_b, small = enter(step_size, latent, time_embed)
    from_b = pair_up(to_b, CHIPS)
    smalls = [small] + [across(small, k) for k in (1, 2, 3)]
    from_a = pair_up(to_a, CORES)
    prior, to_a, to_b, *tables = run_round(0, lat, from_a, from_b, *smalls, conv_in.transpose(0, 1, 3, 2), conv_mid, conv_out)
    from_b, from_a = pair_up(to_b, CHIPS), pair_up(to_a, CORES)
    prior, to_a, to_b = run_round(1, lat, from_a, from_b, prior, *tables)
    from_b, from_a = pair_up(to_b, CHIPS), pair_up(to_a, CORES)
    pieces = run_round(2, lat, from_a, from_b, prior, *tables)
    got = [pieces[0]] + [across(pieces[k], k) for k in (1, 2, 3)]
    return join(got).reshape(2, C, ROWS, 448)


def solution(mesh):
    in_specs = (P(None, "pix", None), P("tm"), P("tm", None), P(), P(), P())
    out_specs = P("tm", None, "pix", None)
    return jax.shard_map(shards, mesh=mesh, in_specs=in_specs, out_specs=out_specs, check_vma=False)
```

```python
import functools

import jax
import jax.numpy as jnp
from jax import lax
from jax.experimental import pallas as pl
from jax.experimental.pallas import tpu as pltpu
from jax.sharding import PartitionSpec as P

TIMES = 8
C = 16
F = 128
L = 128
ROWS = 4
STARTS = (-1, 105, 215, 321)
SHIFTS = tuple(-start % L for start in STARTS)
CUTS = (114, 224, 334)
BF = jnp.bfloat16
F32 = jnp.float32


VM = pl.BlockSpec(memory_space=pltpu.VMEM)
ANY = pl.BlockSpec(memory_space=pl.ANY)


def by_tm(tm, values):
    return jnp.where(tm == 0, values[0], jnp.where(tm == 1, values[1], jnp.where(tm == 2, values[2], values[3])))


def enter_body(step, latent, embed, lat, to_a, to_b, small, step_s, latent_v, embed_v, sems):
    copies = [pltpu.make_async_copy(x, y, sems.at[i]) for i, (x, y) in enumerate(((latent, latent_v), (embed, embed_v), (step, step_s)))]
    for copy in copies:
        copy.start()
    for copy in copies:
        copy.wait()
    tm, core = lax.axis_index("tm"), lax.axis_index("pix") % 2
    shift = by_tm(tm, SHIFTS)
    lane = lax.broadcasted_iota(jnp.int32, (C, L), 1)
    for r in range(ROWS):
        tiles = [jnp.zeros((C, L), F32)] + [latent_v[:, r, g * L:(g + 1) * L] for g in range(3)]
        tiles.append(jnp.concatenate([latent_v[:, r, 3 * L:], jnp.zeros((C, 4 * L - 448), F32)], axis=1))
        left, right = by_tm(tm, tiles[:4]), by_tm(tm, tiles[1:])
        lat[r + core * (3 - 2 * r)] = jnp.where(lane < shift, pltpu.roll(left, shift, 1), pltpu.roll(right, shift, 1))
    for d in range(3):
        to_b[d] = lat[d].astype(BF)
        to_a[d] = lat[3 - d].astype(BF)
    small[0:2] = embed_v[...]
    for d in range(2):
        small[2 + d:3 + d] = jnp.full((1, F), step_s[d], F32)


def enter(step, latent, embed):
    sent = jax.ShapeDtypeStruct((3, C, L), BF)
    return pl.pallas_call(
        enter_body,
        out_shape=(jax.ShapeDtypeStruct((ROWS, C, L), F32), sent, sent, jax.ShapeDtypeStruct((4, F), F32)),
        in_specs=[ANY] * 3,
        out_specs=(VM,) * 4,
        scratch_shapes=[
            pltpu.SMEM((2,), F32),
            pltpu.VMEM((C, ROWS, 448), F32),
            pltpu.VMEM((2, F), F32),
            pltpu.SemaphoreType.DMA((3,)),
        ],
        compiler_params=pltpu.CompilerParams(vmem_limit_bytes=4 << 20),
        name="enter",
    )(step, latent, embed)


def prepare_body(conv_in, conv_mid, conv_out, w_in, w_mid, w_out, in_v, mid_v, out_v, turned, sems):
    copies = [pltpu.make_async_copy(x, y, sems.at[i]) for i, (x, y) in enumerate(((conv_in, in_v), (conv_mid, mid_v), (conv_out, out_v)))]
    for copy in copies:
        copy.start()
    core = lax.axis_index("pix") % 2
    w_mid[...] = jnp.zeros_like(w_mid)
    w_out[...] = jnp.zeros_like(w_out)
    turned[...] = jnp.zeros_like(turned)
    for copy in copies:
        copy.wait()
    for a in range(3):
        row = a + core * (2 - 2 * a)
        for b in range(3):
            mid = mid_v[row, b] * 0.5
            tail = out_v[row, b]
            head = in_v[row, b] * 0.5
            for q in range(2):
                w_mid[(b * 2 + q) * F:(b * 2 + q + 1) * F, (a + q) * F:(a + q + 1) * F] = mid
                w_out[q * 48 + b * C:q * 48 + (b + 1) * C, (a + q) * F:(a + q + 1) * F] = tail
                turned[(a + q) * 48 + b * C:(a + q) * 48 + (b + 1) * C, q * F:(q + 1) * F] = head
    w_in[:2 * F] = turned[...].astype(F32).T.astype(BF)
    w_in[2 * F:] = jnp.zeros((F, 2 * F), BF)


def prepare(conv_in, conv_mid, conv_out):
    shapes = ((3 * F, 2 * F), (7 * F, 4 * F), (96, 4 * F))
    return pl.pallas_call(
        prepare_body,
        out_shape=tuple(jax.ShapeDtypeStruct(shape, BF) for shape in shapes),
        in_specs=[ANY] * 3,
        out_specs=(VM,) * 3,
        scratch_shapes=[
            pltpu.VMEM((3, 3, C, F), BF),
            pltpu.VMEM((3, 3, F, F), BF),
            pltpu.VMEM((3, 3, C, F), BF),
            pltpu.VMEM((2 * F, 2 * F), BF),
            pltpu.SemaphoreType.DMA((3,)),
        ],
        compiler_params=pltpu.CompilerParams(vmem_limit_bytes=8 << 20),
        name="prepare",
    )(conv_in, conv_mid, conv_out)


def tables(tm, smalls, w_conv, w_in, steps, gathered):
    for k in range(4):
        gathered[tm ^ k] = smalls[k][...]
    embed = jnp.concatenate([gathered[t, 0:2] for t in range(4)], axis=0) * 0.5
    steps[...] = jnp.concatenate([gathered[t, 2:4] for t in range(4)], axis=0)
    high = embed.astype(BF).astype(F32)
    rest = embed - high
    middle = rest.astype(BF).astype(F32)
    tail = jnp.concatenate([jnp.zeros((64, F), F32), high, middle, rest - middle, jnp.zeros((40, F), F32)], axis=0)
    tail = tail.T.astype(BF)
    w_in[:, :F] = w_conv[:, :F]
    for q in range(2):
        w_in[q * F:(q + 1) * F, F:] = w_conv[q * F:(q + 1) * F, F:] + tail
    w_in[2 * F:, F:] = w_conv[2 * F:, F:]


def silu2(v):
    return v + v * jnp.tanh(v)


def groups_of(rounds):
    return [(t0, min(4, TIMES - t0)) for t0 in (rounds, rounds + 4)]


class Round:
    def __init__(self, rounds, lat, prior, halo, w_in, w_mid, low, hid, sec):
        self.rounds, self.lat, self.prior, self.halo = rounds, lat, prior, halo
        self.w_in, self.w_mid, self.low, self.hid, self.sec = w_in, w_mid, low, hid, sec
        pix, self.tm = lax.axis_index("pix"), lax.axis_index("tm")
        self.core = pix % 2
        self.inside = (pix > 0) & (pix < 63)
        self.groups = groups_of(rounds)
        lane = lax.broadcasted_iota(jnp.int32, (C, L), 1)
        self.column = jnp.where(((self.tm == 0) & (lane == 0)) | ((self.tm == 3) & (lane == L - 1)), 0.0, 1.0)

    def state(self, t, row):
        return self.lat[row] if self.rounds == 0 else self.prior[t, row]

    def fill(self, g, rows):
        t0, n = self.groups[g]
        rounds, column = self.rounds, self.column
        for w in rows:
            for i in range(n if rounds else 1):
                if 3 <= w < 7:
                    x = self.state(t0 + i, w - 3)
                else:
                    d = 2 - w if w < 3 else w - 7
                    x = self.halo[(t0 + i - rounds, d) if rounds else (d,)].astype(F32)
                x = x * column
                x = jnp.concatenate([pltpu.roll(x, 1, 1) * column, x, pltpu.roll(x, L - 1, 1) * column], axis=0).astype(BF)
                for lanes in ([i] if rounds else range(n)):
                    self.low[g][(w - rows[0]) * 48:(w - rows[0] + 1) * 48, lanes * L:(lanes + 1) * L] = x

    def hidden_pair(self, g, p, first_row):
        t0, n = self.groups[g]
        width = n * L
        r = lax.broadcasted_iota(jnp.int32, (64, width), 0)
        c = lax.broadcasted_iota(jnp.int32, (64, width), 1)
        edge = ((self.tm == 0) & ((c & 127) == 0)) | ((self.tm == 3) & ((c & 127) == L - 1))
        pick = jnp.where(((r & 7) == t0 + (c >> 7)) & (r < 24) & jnp.logical_not(edge), 1.0, 0.0).astype(BF)
        at = (2 * p - first_row) * 48
        rhs = jnp.concatenate([self.low[g][at:at + 192, :width], pick], axis=0)
        w = self.w_in[:2 * F]
        if p == 0:
            w = jnp.concatenate([self.w_in[pl.ds(self.block(q, 2), F), :] for q in range(2)], axis=0)
        v = silu2(jnp.dot(w, rhs, preferred_element_type=F32))
        self.hid(g, p)[:, :width] = v.astype(BF)

    def block(self, normal, zero):
        return pl.multiple_of(jnp.where(self.inside, normal * F, zero * F), F)

    def second_pair(self, g, p):
        _, n = self.groups[g]
        w = self.w_mid[:6 * F]
        if p == 0:
            blocks = []
            for b in range(3):
                blocks += [self.w_mid[pl.ds(self.block(2 * b, 6), F), :], self.w_mid[(2 * b + 1) * F:(2 * b + 2) * F]]
            w = jnp.concatenate(blocks, axis=0)
        for i0 in range(0, n, 2):
            lanes = slice(i0 * L, min(i0 + 2, n) * L)
            rhs = jnp.concatenate([self.hid(g, p)[:, lanes], self.hid(g, p + 1)[:, lanes]], axis=0)
            y = jnp.dot(w, rhs, preferred_element_type=F32)
            for i in range(i0, min(i0 + 2, n)):
                part = y[:, (i - i0) * L:(i - i0 + 1) * L]
                v = pltpu.roll(part[:2 * F], 1, 1) + part[2 * F:4 * F] + pltpu.roll(part[4 * F:], L - 1, 1)
                self.sec(g, p)[:, i * L:(i + 1) * L] = silu2(v).astype(BF)


def first_part(rounds, *refs):
    if rounds == 0:
        lat, from_a, *smalls = refs[:6]
        w_conv, w_mid, h0, h1, s0, s1, w_in, steps, low0, low1, h3_0, h3_1, gathered = refs[6:]
        tables(lax.axis_index("tm"), smalls, w_conv, w_in, steps, gathered)
        prior = None
    else:
        lat, from_a, prior, w_in, w_mid, h0, h1, s0, s1, low0, low1, h3_0, h3_1 = refs
    r = Round(rounds, lat, prior, from_a, w_in, w_mid, (low0, low1), lambda g, p: ((h0, h1), (h3_0, h3_1))[p - 2][g], lambda g, p: (s0, s1)[g])
    rows = list(range(4, 10))
    for g in range(2):
        r.fill(g, rows)
        r.hidden_pair(g, 2, 4)
        r.hidden_pair(g, 3, 4)
    for g in range(2):
        r.second_pair(g, 2)


def second_part(rounds, *refs):
    lat, from_b = refs[:2]
    prior = refs[2] if rounds else None
    h0, h1, s0, s1, w_in, w_mid, w_out, steps, *rest = refs[3 if rounds else 2:]
    last = rounds == 2
    if last:
        out, rest = rest[:4], rest[4:]
        ready = rest.pop()
    else:
        nxt, to_a, to_b, *rest = rest
    low, hid, sec = rest[:2], rest[2:6], rest[6:10]
    r = Round(rounds, lat, prior, from_b, w_in, w_mid, low, lambda g, p: hid[g * 2 + p] if p < 2 else (h0, h1)[g], lambda g, p: sec[g * 2 + p] if p < 2 else (s0, s1)[g])
    core, tm, column = r.core, r.tm, r.column

    def keep(t, row, value):
        ready[pl.ds(((t // 2) ^ tm) * 128 + (t % 2) * 64 + row + core * (3 - 2 * row), C, stride=ROWS), :] = value

    totals = [jnp.zeros((C, L), F32) if rounds == 0 else prior[0, row] for row in range(ROWS)]

    def out_pair(g, p):
        t0, n = r.groups[g]
        width = n * L
        rhs = jnp.concatenate([r.sec(g, p)[:, :width], r.sec(g, p + 1)[:, :width]], axis=0)
        y = jnp.dot(w_out[...], rhs, preferred_element_type=F32)
        for q in range(2):
            row = 2 * p + q
            for i in range(n):
                t = t0 + i
                part = y[q * 48:(q + 1) * 48, i * L:(i + 1) * L]
                conv = pltpu.roll(part[:C] * column, 1, 1) + part[C:2 * C] + pltpu.roll(part[2 * C:] * column, L - 1, 1)
                totals[row] = totals[row] + steps[t:t + 1] * (r.state(t, row) + conv)
                value = lat[row] + totals[row]
                if last:
                    keep(t, row, value)
                else:
                    nxt[t + 1, row] = value
                    if t == rounds:
                        nxt[0, row] = totals[row]
                    if t < TIMES - 1 and row < 3:
                        to_b[t - rounds, row] = value.astype(BF)
                    if t < TIMES - 1 and row > 0:
                        to_a[t - rounds, 3 - row] = value.astype(BF)

    rows = list(range(6))
    r.fill(0, rows)
    r.hidden_pair(0, 0, 0)
    r.hidden_pair(0, 1, 0)
    r.fill(1, rows)
    r.second_pair(0, 1)
    r.hidden_pair(1, 1, 0)
    r.second_pair(0, 0)
    r.hidden_pair(1, 0, 0)
    out_pair(0, 1)
    out_pair(0, 0)
    r.second_pair(1, 1)
    out_pair(1, 1)
    r.second_pair(1, 0)
    out_pair(1, 0)

    for row in range(ROWS):
        if rounds == 1:
            nxt[1, row] = prior[1, row]
        if last:
            for t in range(2):
                keep(t, row, prior[t + 1, row])
    if last:
        for k in range(4):
            out[k][...] = ready[k * 128:(k + 1) * 128].reshape(32, ROWS, L)


def call(body, rounds, args, out_shape, scratch):
    return pl.pallas_call(
        functools.partial(body, rounds),
        out_shape=out_shape,
        in_specs=[VM] * len(args),
        out_specs=(VM,) * len(out_shape),
        scratch_shapes=scratch,
        compiler_params=pltpu.CompilerParams(vmem_limit_bytes=24 << 20),
    )(*args)


PAIR = (2 * F, 4 * L)
LOW = [pltpu.VMEM((288, 4 * L), BF)] * 2


def run_first(rounds, *args):
    out_shape = (jax.ShapeDtypeStruct(PAIR, BF),) * 4
    scratch = LOW + [pltpu.VMEM(PAIR, BF)] * 2
    if rounds == 0:
        out_shape += (jax.ShapeDtypeStruct((3 * F, 2 * F), BF), jax.ShapeDtypeStruct((TIMES, F), F32))
        scratch += [pltpu.VMEM((4, 4, F), F32)]
    return call(first_part, rounds, args, out_shape, scratch)


def run_second(rounds, *args):
    scratch = LOW + [pltpu.VMEM(PAIR, BF)] * 8
    if rounds == 2:
        out_shape = (jax.ShapeDtypeStruct((32, ROWS, L), F32),) * 4
        scratch += [pltpu.VMEM((512, L), F32)]
    else:
        sent = jax.ShapeDtypeStruct((TIMES - 1 - rounds, 3, C, L), BF)
        out_shape = (jax.ShapeDtypeStruct((TIMES + 1, ROWS, C, L), F32), sent, sent)
    return call(second_part, rounds, args, out_shape, scratch)


def join_body(p0, p1, p2, p3, out):
    tm = lax.axis_index("tm")
    pieces = [p0[...], p1[...], p2[...], p3[...]]
    lane = lax.broadcasted_iota(jnp.int32, pieces[0].shape, 2)
    placed = []
    for t in range(4):
        x = by_tm(t ^ tm, pieces)
        placed.append(pltpu.roll(x, STARTS[t] % L, 2))
    for g in range(3):
        out[:, :, g * L:(g + 1) * L] = jnp.where(lane < CUTS[g] - g * L, placed[g], placed[g + 1])
    out[:, :, 3 * L:] = placed[3][:, :, :448 - 3 * L]


def join(pieces):
    return pl.pallas_call(
        join_body,
        out_shape=jax.ShapeDtypeStruct((32, ROWS, 448), F32),
        in_specs=[VM] * 4,
        out_specs=VM,
        compiler_params=pltpu.CompilerParams(vmem_limit_bytes=8 << 20),
        name="join",
    )(*pieces)


def across(x, k):
    return lax.ppermute(x, "tm", [(t, t ^ k) for t in range(4)])


def pair_up(x, pairs):
    return lax.ppermute(x, "pix", [(a, b) for a, b in pairs] + [(b, a) for a, b in pairs])


CORES = [(2 * k, 2 * k + 1) for k in range(32)]
CHIPS = [(2 * k + 1, 2 * k + 2) for k in range(31)]


def shards(latent, step_size, time_embed, conv_in, conv_mid, conv_out):
    lat, to_a, to_b, small = enter(step_size, latent, time_embed)
    smalls = [small]
    for k in (1, 2, 3):
        smalls.append(across(small, k))
    w_conv, w_mid, w_out = prepare(conv_in.transpose(0, 1, 3, 2), conv_mid, conv_out)
    prior = ()
    for rounds in range(3):
        from_b = pair_up(to_b, CHIPS)
        from_a = pair_up(to_a, CORES)
        if rounds == 0:
            *kept, w_in, steps = run_first(0, lat, from_a, *smalls, w_conv, w_mid)
        else:
            kept = run_first(rounds, lat, from_a, *prior, w_in, w_mid)
        done = run_second(rounds, lat, from_b, *prior, *kept, w_in, w_mid, w_out, steps)
        if rounds < 2:
            *prior, to_a, to_b = done
    got = [done[0]] + [across(done[k], k) for k in (1, 2, 3)]
    return join(got).reshape(2, C, ROWS, 448)


def solution(mesh):
    in_specs = (P(None, "pix", None), P("tm"), P("tm", None), P(), P(), P())
    out_specs = P("tm", None, "pix", None)
    return jax.shard_map(shards, mesh=mesh, in_specs=in_specs, out_specs=out_specs, check_vma=False)
```

```python
import functools

import jax
import jax.numpy as jnp
from jax import lax
from jax.experimental import pallas as pl
from jax.experimental.pallas import tpu as pltpu
from jax.sharding import PartitionSpec as P


TIMES = 8
C = 16
F = 128
L = 128
ROWS = 4
STARTS = (-1, 105, 215, 321)
SHIFTS = tuple(-start % L for start in STARTS)
CUTS = (114, 224, 334)
BF = jnp.bfloat16
F32 = jnp.float32


VM = pl.BlockSpec(memory_space=pltpu.VMEM)
ANY = pl.BlockSpec(memory_space=pltpu.HBM)


def by_tm(tm, values):
    return jnp.where(tm == 0, values[0], jnp.where(tm == 1, values[1], jnp.where(tm == 2, values[2], values[3])))


def enter_body(step, latent, embed, lat, to_a, to_b, small, step_s, latent_v, embed_v, sems):
    copies = [pltpu.make_async_copy(x, y, sems.at[i]) for i, (x, y) in enumerate(((latent, latent_v), (embed, embed_v), (step, step_s)))]
    for copy in copies:
        copy.start()
    for copy in copies:
        copy.wait()
    tm, core = lax.axis_index("tm"), lax.axis_index("pix") % 2
    shift = by_tm(tm, SHIFTS)
    lane = lax.broadcasted_iota(jnp.int32, (C, L), 1)
    for r in range(ROWS):
        tiles = [jnp.zeros((C, L), F32)] + [latent_v[:, r, g * L:(g + 1) * L] for g in range(3)]
        tiles.append(jnp.concatenate([latent_v[:, r, 3 * L:], jnp.zeros((C, 4 * L - 448), F32)], axis=1))
        left, right = by_tm(tm, tiles[:4]), by_tm(tm, tiles[1:])
        lat[r + core * (3 - 2 * r)] = jnp.where(lane < shift, pltpu.roll(left, shift, 1), pltpu.roll(right, shift, 1))
    for d in range(3):
        to_b[d] = lat[d].astype(BF)
        to_a[d] = lat[3 - d].astype(BF)
    small[0:2] = embed_v[...]
    for d in range(2):
        small[2 + d:3 + d] = jnp.full((1, F), step_s[d], F32)


def enter(step, latent, embed):
    sent = jax.ShapeDtypeStruct((3, C, L), BF)
    return pl.pallas_call(
        enter_body,
        out_shape=(jax.ShapeDtypeStruct((ROWS, C, L), F32), sent, sent, jax.ShapeDtypeStruct((4, F), F32)),
        in_specs=[ANY] * 3,
        out_specs=(VM,) * 4,
        scratch_shapes=[
            pltpu.SMEM((2,), F32),
            pltpu.VMEM((C, ROWS, 448), F32),
            pltpu.VMEM((2, F), F32),
            pltpu.SemaphoreType.DMA((3,)),
        ],
        compiler_params=pltpu.CompilerParams(vmem_limit_bytes=4 << 20),
        name="enter",
    )(*[pltpu.with_memory_space_constraint(v, pltpu.HBM) for v in (step, latent, embed)])


def prepare_body(conv_in, conv_mid, conv_out, w_in, w_mid, w_out, in_v, mid_v, out_v, turned, sems):
    copies = [pltpu.make_async_copy(x, y, sems.at[i]) for i, (x, y) in enumerate(((conv_in, in_v), (conv_mid, mid_v), (conv_out, out_v)))]
    for copy in copies:
        copy.start()
    core = lax.axis_index("pix") % 2
    w_mid[...] = jnp.zeros_like(w_mid)
    w_out[...] = jnp.zeros_like(w_out)
    turned[...] = jnp.zeros_like(turned)
    for copy in copies:
        copy.wait()
    for a in range(3):
        row = a + core * (2 - 2 * a)
        for b in range(3):
            mid = mid_v[row, b] * 0.5
            tail = out_v[row, b]
            head = in_v[row, b] * 0.5
            for q in range(2):
                w_mid[(b * 2 + q) * F:(b * 2 + q + 1) * F, (a + q) * F:(a + q + 1) * F] = mid
                w_out[q * 48 + b * C:q * 48 + (b + 1) * C, (a + q) * F:(a + q + 1) * F] = tail
                turned[(a + q) * 48 + b * C:(a + q) * 48 + (b + 1) * C, q * F:(q + 1) * F] = head
    w_in[:2 * F] = turned[...].astype(F32).T.astype(BF)
    w_in[2 * F:] = jnp.zeros((F, 2 * F), BF)


def prepare(conv_in, conv_mid, conv_out):
    shapes = ((3 * F, 2 * F), (7 * F, 4 * F), (96, 4 * F))
    return pl.pallas_call(
        prepare_body,
        out_shape=tuple(jax.ShapeDtypeStruct(shape, BF) for shape in shapes),
        in_specs=[ANY] * 3,
        out_specs=(VM,) * 3,
        scratch_shapes=[
            pltpu.VMEM((3, 3, C, F), BF),
            pltpu.VMEM((3, 3, F, F), BF),
            pltpu.VMEM((3, 3, C, F), BF),
            pltpu.VMEM((2 * F, 2 * F), BF),
            pltpu.SemaphoreType.DMA((3,)),
        ],
        compiler_params=pltpu.CompilerParams(vmem_limit_bytes=8 << 20),
        name="prepare",
    )(*[pltpu.with_memory_space_constraint(v, pltpu.HBM) for v in (conv_in, conv_mid, conv_out)])


def tables(tm, smalls, w_conv, w_in, steps, gathered):
    for k in range(4):
        gathered[tm ^ k] = smalls[k][...]
    embed = jnp.concatenate([gathered[t, 0:2] for t in range(4)], axis=0) * 0.5
    steps[...] = jnp.concatenate([gathered[t, 2:4] for t in range(4)], axis=0)
    high = embed.astype(BF).astype(F32)
    rest = embed - high
    middle = rest.astype(BF).astype(F32)
    tail = jnp.concatenate([jnp.zeros((64, F), F32), high, middle, rest - middle, jnp.zeros((40, F), F32)], axis=0)
    tail = tail.T.astype(BF)
    w_in[:, :F] = w_conv[:, :F]
    for q in range(2):
        w_in[q * F:(q + 1) * F, F:] = w_conv[q * F:(q + 1) * F, F:] + tail
    w_in[2 * F:, F:] = w_conv[2 * F:, F:]


def silu2(v):
    return v + v * jnp.tanh(v)


def groups_of(rounds):
    return [(t0, min(4, TIMES - t0)) for t0 in (rounds, rounds + 4)]


class Round:
    def __init__(self, rounds, lat, prior, halo, w_in, w_mid, low, hid, sec):
        self.rounds, self.lat, self.prior, self.halo = rounds, lat, prior, halo
        self.w_in, self.w_mid, self.low, self.hid, self.sec = w_in, w_mid, low, hid, sec
        pix, self.tm = lax.axis_index("pix"), lax.axis_index("tm")
        self.core = pix % 2
        self.inside = (pix > 0) & (pix < 63)
        self.groups = groups_of(rounds)
        lane = lax.broadcasted_iota(jnp.int32, (C, L), 1)
        self.column = jnp.where(((self.tm == 0) & (lane == 0)) | ((self.tm == 3) & (lane == L - 1)), 0.0, 1.0)

    def state(self, t, row):
        return self.lat[row] if self.rounds == 0 else self.prior[t, row]

    def fill(self, g, rows):
        t0, n = self.groups[g]
        rounds, column = self.rounds, self.column
        for w in rows:
            for i in range(n if rounds else 1):
                if 3 <= w < 7:
                    x = self.state(t0 + i, w - 3)
                else:
                    d = 2 - w if w < 3 else w - 7
                    x = self.halo[(t0 + i - rounds, d) if rounds else (d,)].astype(F32)
                x = x * column
                x = jnp.concatenate([pltpu.roll(x, 1, 1) * column, x, pltpu.roll(x, L - 1, 1) * column], axis=0).astype(BF)
                for lanes in ([i] if rounds else range(n)):
                    self.low[g][(w - rows[0]) * 48:(w - rows[0] + 1) * 48, lanes * L:(lanes + 1) * L] = x

    def hidden_pair(self, g, p, first_row):
        t0, n = self.groups[g]
        width = n * L
        r = lax.broadcasted_iota(jnp.int32, (64, width), 0)
        c = lax.broadcasted_iota(jnp.int32, (64, width), 1)
        edge = ((self.tm == 0) & ((c & 127) == 0)) | ((self.tm == 3) & ((c & 127) == L - 1))
        pick = jnp.where(((r & 7) == t0 + (c >> 7)) & (r < 24) & jnp.logical_not(edge), 1.0, 0.0).astype(BF)
        at = (2 * p - first_row) * 48
        rhs = jnp.concatenate([self.low[g][at:at + 192, :width], pick], axis=0)
        w = self.w_in[:2 * F]
        if p == 0:
            w = jnp.concatenate([self.w_in[pl.ds(self.block(q, 2), F), :] for q in range(2)], axis=0)
        v = silu2(jnp.dot(w, rhs, preferred_element_type=F32))
        self.hid(g, p)[:, :width] = v.astype(BF)

    def block(self, normal, zero):
        return pl.multiple_of(jnp.where(self.inside, normal * F, zero * F), F)

    def second_pair(self, g, p):
        _, n = self.groups[g]
        w = self.w_mid[:6 * F]
        if p == 0:
            blocks = []
            for b in range(3):
                blocks += [self.w_mid[pl.ds(self.block(2 * b, 6), F), :], self.w_mid[(2 * b + 1) * F:(2 * b + 2) * F]]
            w = jnp.concatenate(blocks, axis=0)
        for i0 in range(0, n, 2):
            lanes = slice(i0 * L, min(i0 + 2, n) * L)
            rhs = jnp.concatenate([self.hid(g, p)[:, lanes], self.hid(g, p + 1)[:, lanes]], axis=0)
            y = jnp.dot(w, rhs, preferred_element_type=F32)
            for i in range(i0, min(i0 + 2, n)):
                part = y[:, (i - i0) * L:(i - i0 + 1) * L]
                v = pltpu.roll(part[:2 * F], 1, 1) + part[2 * F:4 * F] + pltpu.roll(part[4 * F:], L - 1, 1)
                self.sec(g, p)[:, i * L:(i + 1) * L] = silu2(v).astype(BF)


def first_part(rounds, *refs):
    if rounds == 0:
        lat, from_a, *smalls = refs[:6]
        w_conv, w_mid, h0, h1, s0, s1, w_in, steps, low0, low1, h3_0, h3_1, gathered = refs[6:]
        tables(lax.axis_index("tm"), smalls, w_conv, w_in, steps, gathered)
        prior = None
    else:
        lat, from_a, prior, w_in, w_mid, h0, h1, s0, s1, low0, low1, h3_0, h3_1 = refs
    r = Round(rounds, lat, prior, from_a, w_in, w_mid, (low0, low1), lambda g, p: ((h0, h1), (h3_0, h3_1))[p - 2][g], lambda g, p: (s0, s1)[g])
    rows = list(range(4, 10))
    for g in range(2):
        r.fill(g, rows)
        r.hidden_pair(g, 2, 4)
        r.hidden_pair(g, 3, 4)
    for g in range(2):
        r.second_pair(g, 2)


def second_part(rounds, *refs):
    lat, from_b = refs[:2]
    prior = refs[2] if rounds else None
    h0, h1, s0, s1, w_in, w_mid, w_out, steps, *rest = refs[3 if rounds else 2:]
    last = rounds == 2
    if last:
        out, rest = rest[:4], rest[4:]
        ready = rest.pop()
    else:
        nxt, to_a, to_b, *rest = rest
    low, hid, sec = rest[:2], rest[2:6], rest[6:10]
    r = Round(rounds, lat, prior, from_b, w_in, w_mid, low, lambda g, p: hid[g * 2 + p] if p < 2 else (h0, h1)[g], lambda g, p: sec[g * 2 + p] if p < 2 else (s0, s1)[g])
    core, tm, column = r.core, r.tm, r.column

    def keep(t, row, value):
        ready[pl.ds(((t // 2) ^ tm) * 128 + (t % 2) * 64 + row + core * (3 - 2 * row), C, stride=ROWS), :] = value

    totals = [jnp.zeros((C, L), F32) if rounds == 0 else prior[0, row] for row in range(ROWS)]

    def out_pair(g, p):
        t0, n = r.groups[g]
        width = n * L
        rhs = jnp.concatenate([r.sec(g, p)[:, :width], r.sec(g, p + 1)[:, :width]], axis=0)
        y = jnp.dot(w_out[...], rhs, preferred_element_type=F32)
        for q in range(2):
            row = 2 * p + q
            for i in range(n):
                t = t0 + i
                part = y[q * 48:(q + 1) * 48, i * L:(i + 1) * L]
                conv = pltpu.roll(part[:C] * column, 1, 1) + part[C:2 * C] + pltpu.roll(part[2 * C:] * column, L - 1, 1)
                totals[row] = totals[row] + steps[t:t + 1] * (r.state(t, row) + conv)
                value = lat[row] + totals[row]
                if last:
                    keep(t, row, value)
                else:
                    nxt[t + 1, row] = value
                    if t == rounds:
                        nxt[0, row] = totals[row]
                    if t < TIMES - 1 and row < 3:
                        to_b[t - rounds, row] = value.astype(BF)
                    if t < TIMES - 1 and row > 0:
                        to_a[t - rounds, 3 - row] = value.astype(BF)

    rows = list(range(6))
    r.fill(0, rows)
    r.hidden_pair(0, 0, 0)
    r.hidden_pair(0, 1, 0)
    r.fill(1, rows)
    r.second_pair(0, 1)
    r.hidden_pair(1, 1, 0)
    r.second_pair(0, 0)
    r.hidden_pair(1, 0, 0)
    out_pair(0, 1)
    out_pair(0, 0)
    r.second_pair(1, 1)
    out_pair(1, 1)
    r.second_pair(1, 0)
    out_pair(1, 0)

    for row in range(ROWS):
        if rounds == 1:
            nxt[1, row] = prior[1, row]
        if last:
            for t in range(2):
                keep(t, row, prior[t + 1, row])
    if last:
        for k in range(4):
            out[k][...] = ready[k * 128:(k + 1) * 128].reshape(32, ROWS, L)


def call(body, rounds, args, out_shape, scratch):
    return pl.pallas_call(
        functools.partial(body, rounds),
        out_shape=out_shape,
        in_specs=[VM] * len(args),
        out_specs=(VM,) * len(out_shape),
        scratch_shapes=scratch,
        compiler_params=pltpu.CompilerParams(vmem_limit_bytes=24 << 20),
    )(*args)


PAIR = (2 * F, 4 * L)
LOW = [pltpu.VMEM((288, 4 * L), BF)] * 2


def run_first(rounds, *args):
    out_shape = (jax.ShapeDtypeStruct(PAIR, BF),) * 4
    scratch = LOW + [pltpu.VMEM(PAIR, BF)] * 2
    if rounds == 0:
        out_shape += (jax.ShapeDtypeStruct((3 * F, 2 * F), BF), jax.ShapeDtypeStruct((TIMES, F), F32))
        scratch += [pltpu.VMEM((4, 4, F), F32)]
    return call(first_part, rounds, args, out_shape, scratch)


def run_second(rounds, *args):
    scratch = LOW + [pltpu.VMEM(PAIR, BF)] * 8
    if rounds == 2:
        out_shape = (jax.ShapeDtypeStruct((32, ROWS, L), F32),) * 4
        scratch += [pltpu.VMEM((512, L), F32)]
    else:
        sent = jax.ShapeDtypeStruct((TIMES - 1 - rounds, 3, C, L), BF)
        out_shape = (jax.ShapeDtypeStruct((TIMES + 1, ROWS, C, L), F32), sent, sent)
    return call(second_part, rounds, args, out_shape, scratch)


def join_body(p0, p1, p2, p3, out):
    tm = lax.axis_index("tm")
    pieces = [p0[...], p1[...], p2[...], p3[...]]
    lane = lax.broadcasted_iota(jnp.int32, pieces[0].shape, 2)
    placed = []
    for t in range(4):
        x = by_tm(t ^ tm, pieces)
        placed.append(pltpu.roll(x, STARTS[t] % L, 2))
    for g in range(3):
        out[:, :, g * L:(g + 1) * L] = jnp.where(lane < CUTS[g] - g * L, placed[g], placed[g + 1])
    out[:, :, 3 * L:] = placed[3][:, :, :448 - 3 * L]


def join(pieces):
    return pl.pallas_call(
        join_body,
        out_shape=jax.ShapeDtypeStruct((32, ROWS, 448), F32),
        in_specs=[VM] * 4,
        out_specs=VM,
        compiler_params=pltpu.CompilerParams(vmem_limit_bytes=8 << 20),
        name="join",
    )(*pieces)


def across(x, k):
    return lax.ppermute(x, "tm", [(t, t ^ k) for t in range(4)])


def pair_up(x, pairs):
    return lax.ppermute(x, "pix", [(a, b) for a, b in pairs] + [(b, a) for a, b in pairs])


CORES = [(2 * k, 2 * k + 1) for k in range(32)]
CHIPS = [(2 * k + 1, 2 * k + 2) for k in range(31)]


def shards(latent, step_size, time_embed, conv_in, conv_mid, conv_out):
    lat, to_a, to_b, small = enter(step_size, latent, time_embed)
    smalls = [small]
    for k in (1, 2, 3):
        smalls.append(across(small, k))
    w_conv, w_mid, w_out = prepare(conv_in.transpose(0, 1, 3, 2), conv_mid, conv_out)
    prior = ()
    for rounds in range(3):
        from_b = pair_up(to_b, CHIPS)
        from_a = pair_up(to_a, CORES)
        if rounds == 0:
            *kept, w_in, steps = run_first(0, lat, from_a, *smalls, w_conv, w_mid)
        else:
            kept = run_first(rounds, lat, from_a, *prior, w_in, w_mid)
        done = run_second(rounds, lat, from_b, *prior, *kept, w_in, w_mid, w_out, steps)
        if rounds < 2:
            *prior, to_a, to_b = done
    got = [done[0]] + [across(done[k], k) for k in (1, 2, 3)]
    return join(got).reshape(2, C, ROWS, 448)


def solution(mesh):
    in_specs = (P(None, "pix", None), P("tm"), P("tm", None), P(), P(), P())
    out_specs = P("tm", None, "pix", None)
    return jax.shard_map(shards, mesh=mesh, in_specs=in_specs, out_specs=out_specs, check_vma=False)
```

```python
import functools

import jax
import jax.numpy as jnp
from jax import lax
from jax.experimental import pallas as pl
from jax.experimental.pallas import tpu as pltpu
from jax.sharding import PartitionSpec as P


TIMES = 8
C = 16
F = 128
L = 128
ROWS = 4
STARTS = (-1, 105, 215, 321)
SHIFTS = tuple(-start % L for start in STARTS)
CUTS = (114, 224, 334)
BF = jnp.bfloat16
F32 = jnp.float32


VM = pl.BlockSpec(memory_space=pltpu.VMEM)
ANY = pl.BlockSpec(memory_space=pltpu.HBM)


def by_tm(tm, values):
    return jnp.where(tm == 0, values[0], jnp.where(tm == 1, values[1], jnp.where(tm == 2, values[2], values[3])))


def pieces_of(x):
    high = x.astype(BF).astype(F32)
    rest = x - high
    middle = rest.astype(BF).astype(F32)
    return high, middle, rest - middle


def enter_body(step, latent, embed, lat, to_a, to_b, small, step_s, latent_v, embed_v, other, sems):
    copies = [pltpu.make_async_copy(x, y, sems.at[i]) for i, (x, y) in enumerate(((latent, latent_v), (embed, embed_v), (step, step_s)))]
    for copy in copies:
        copy.start()
    for copy in copies:
        copy.wait()
    tm, core = lax.axis_index("tm"), lax.axis_index("pix") % 2
    lane = lax.broadcasted_iota(jnp.int32, (C, L), 1)
    for r in range(ROWS):
        tiles = [jnp.zeros((C, L), F32)] + [latent_v[:, r, g * L:(g + 1) * L] for g in range(3)]
        tiles.append(jnp.concatenate([latent_v[:, r, 3 * L:], jnp.zeros((C, 4 * L - 448), F32)], axis=1))
        for t, to in ((tm, lat), (tm ^ 2, other)):
            shift = by_tm(t, SHIFTS)
            left, right = by_tm(t, tiles[:4]), by_tm(t, tiles[1:])
            to[r + core * (3 - 2 * r)] = jnp.where(lane < shift, pltpu.roll(left, shift, 1), pltpu.roll(right, shift, 1))
    for d in range(3):
        to_b[d] = lat[d].astype(BF)
        to_a[d] = other[3 - d].astype(BF)
    rows = jnp.concatenate([embed_v[...]] + [jnp.full((1, F), step_s[d], F32) for d in range(2)], axis=0)
    table = jnp.concatenate([*pieces_of(rows), jnp.zeros((4, F), F32)], axis=0).astype(BF)
    small[...] = table
    to_a[3] = table


def enter(step, latent, embed):
    shapes = ((4, C, L), (3, C, L), (16, F))
    return pl.pallas_call(
        enter_body,
        out_shape=(jax.ShapeDtypeStruct((ROWS, C, L), F32),) + tuple(jax.ShapeDtypeStruct(shape, BF) for shape in shapes),
        in_specs=[ANY] * 3,
        out_specs=(VM,) * 4,
        scratch_shapes=[
            pltpu.SMEM((2,), F32),
            pltpu.VMEM((C, ROWS, 448), F32),
            pltpu.VMEM((2, F), F32),
            pltpu.VMEM((ROWS, C, L), F32),
            pltpu.SemaphoreType.DMA((3,)),
        ],
        compiler_params=pltpu.CompilerParams(vmem_limit_bytes=4 << 20),
        name="enter",
    )(*[pltpu.with_memory_space_constraint(v, pltpu.HBM) for v in (step, latent, embed)])


def prepare_body(conv_in, conv_mid, conv_out, w_in, w_mid, w_out, in_v, mid_v, out_v, turned, sems):
    copies = [pltpu.make_async_copy(x, y, sems.at[i]) for i, (x, y) in enumerate(((conv_in, in_v), (conv_mid, mid_v), (conv_out, out_v)))]
    for copy in copies:
        copy.start()
    core = lax.axis_index("pix") % 2
    w_mid[...] = jnp.zeros_like(w_mid)
    w_out[...] = jnp.zeros_like(w_out)
    turned[...] = jnp.zeros_like(turned)
    for copy in copies:
        copy.wait()
    for a in range(3):
        row = a + core * (2 - 2 * a)
        for b in range(3):
            mid = mid_v[row, b] * 0.5
            tail = out_v[row, b]
            head = in_v[row, b] * 0.5
            for q in range(2):
                w_mid[(b * 2 + q) * F:(b * 2 + q + 1) * F, (a + q) * F:(a + q + 1) * F] = mid
                w_out[q * 48 + b * C:q * 48 + (b + 1) * C, (a + q) * F:(a + q + 1) * F] = tail
                turned[(a + q) * 48 + b * C:(a + q) * 48 + (b + 1) * C, q * F:(q + 1) * F] = head
    w_in[:2 * F] = turned[...].astype(F32).T.astype(BF)
    w_in[2 * F:] = jnp.zeros((F, 2 * F), BF)


def prepare(conv_in, conv_mid, conv_out):
    shapes = ((3 * F, 2 * F), (7 * F, 4 * F), (96, 4 * F))
    return pl.pallas_call(
        prepare_body,
        out_shape=tuple(jax.ShapeDtypeStruct(shape, BF) for shape in shapes),
        in_specs=[ANY] * 3,
        out_specs=(VM,) * 3,
        scratch_shapes=[
            pltpu.VMEM((3, 3, C, F), BF),
            pltpu.VMEM((3, 3, F, F), BF),
            pltpu.VMEM((3, 3, C, F), BF),
            pltpu.VMEM((2 * F, 2 * F), BF),
            pltpu.SemaphoreType.DMA((3,)),
        ],
        compiler_params=pltpu.CompilerParams(vmem_limit_bytes=8 << 20),
        name="prepare",
    )(*[pltpu.with_memory_space_constraint(v, pltpu.HBM) for v in (conv_in, conv_mid, conv_out)])


def tables(tm, smalls, w_conv, w_in, steps, gathered):
    for k in range(4):
        gathered[tm ^ k] = smalls[k].astype(F32)
    high, middle, rest = [jnp.concatenate([gathered[t, at:at + 2] for t in range(4)], axis=0) * 0.5 for at in (0, 4, 8)]
    steps[...] = sum(jnp.concatenate([gathered[t, at:at + 2] for t in range(4)], axis=0) for at in (2, 6, 10))
    tail = jnp.concatenate([jnp.zeros((64, F), F32), high, middle, rest, jnp.zeros((40, F), F32)], axis=0)
    tail = tail.T.astype(BF)
    w_in[:, :F] = w_conv[:, :F]
    for q in range(2):
        w_in[q * F:(q + 1) * F, F:] = w_conv[q * F:(q + 1) * F, F:] + tail
    w_in[2 * F:, F:] = w_conv[2 * F:, F:]


def silu2(v):
    return v + v * jnp.tanh(v)


def groups_of(rounds):
    return [(t0, min(2, TIMES - t0)) for t0 in range(rounds, TIMES, 2)]


class Round:
    def __init__(self, rounds, lat, prior, halo, w_in, w_mid, low, hid, sec):
        self.rounds, self.lat, self.prior, self.halo = rounds, lat, prior, halo
        self.w_in, self.w_mid, self.low, self.hid, self.sec = w_in, w_mid, low, hid, sec
        pix, self.tm = lax.axis_index("pix"), lax.axis_index("tm")
        self.core = pix % 2
        self.inside = (pix > 0) & (pix < 63)
        self.groups = groups_of(rounds)
        lane = lax.broadcasted_iota(jnp.int32, (C, L), 1)
        self.column = jnp.where(((self.tm == 0) & (lane == 0)) | ((self.tm == 3) & (lane == L - 1)), 0.0, 1.0)

    def state(self, t, row):
        return self.lat[row] if self.rounds == 0 else self.prior[t, row]

    def fill(self, g, rows):
        t0, n = self.groups[g]
        rounds, column = self.rounds, self.column
        for w in rows:
            for i in range(n if rounds else 1):
                if 3 <= w < 7:
                    x = self.state(t0 + i, w - 3)
                else:
                    d = 2 - w if w < 3 else w - 7
                    x = self.halo[(t0 + i - rounds, d) if rounds else (d,)].astype(F32)
                x = x * column
                x = jnp.concatenate([pltpu.roll(x, 1, 1) * column, x, pltpu.roll(x, L - 1, 1) * column], axis=0).astype(BF)
                for lanes in ([i] if rounds else range(n)):
                    self.low[g][(w - rows[0]) * 48:(w - rows[0] + 1) * 48, lanes * L:(lanes + 1) * L] = x

    def hidden_pair(self, g, p, first_row):
        t0, n = self.groups[g]
        width = n * L
        r = lax.broadcasted_iota(jnp.int32, (64, width), 0)
        c = lax.broadcasted_iota(jnp.int32, (64, width), 1)
        edge = ((self.tm == 0) & ((c & 127) == 0)) | ((self.tm == 3) & ((c & 127) == L - 1))
        pick = jnp.where(((r & 7) == t0 + (c >> 7)) & (r < 24) & jnp.logical_not(edge), 1.0, 0.0).astype(BF)
        at = (2 * p - first_row) * 48
        rhs = jnp.concatenate([self.low[g][at:at + 192, :width], pick], axis=0)
        w = self.w_in[:2 * F]
        if p == 0:
            w = jnp.concatenate([self.w_in[pl.ds(self.block(q, 2), F), :] for q in range(2)], axis=0)
        v = silu2(jnp.dot(w, rhs, preferred_element_type=F32))
        self.hid(g, p)[:, :width] = v.astype(BF)

    def block(self, normal, zero):
        return pl.multiple_of(jnp.where(self.inside, normal * F, zero * F), F)

    def second_pair(self, g, p):
        _, n = self.groups[g]
        w = self.w_mid[:6 * F]
        if p == 0:
            blocks = []
            for b in range(3):
                blocks += [self.w_mid[pl.ds(self.block(2 * b, 6), F), :], self.w_mid[(2 * b + 1) * F:(2 * b + 2) * F]]
            w = jnp.concatenate(blocks, axis=0)
        lanes = slice(0, n * L)
        rhs = jnp.concatenate([self.hid(g, p)[:, lanes], self.hid(g, p + 1)[:, lanes]], axis=0)
        y = jnp.dot(w, rhs, preferred_element_type=F32)
        for i in range(n):
            part = y[:, i * L:(i + 1) * L]
            v = pltpu.roll(part[:2 * F], 1, 1) + part[2 * F:4 * F] + pltpu.roll(part[4 * F:], L - 1, 1)
            self.sec(g, p)[:, i * L:(i + 1) * L] = silu2(v).astype(BF)


def first_part(rounds, *refs):
    if rounds == 0:
        lat, from_a, own, one, three, w_conv, w_mid, kept_h, kept_s, w_in, steps, *rest = refs
        smalls = [own[...], one[...], from_a[3], three[...]]
        tables(lax.axis_index("tm"), smalls, w_conv, w_in, steps, rest.pop())
        prior = None
    else:
        lat, from_a, prior, w_in, w_mid, kept_h, kept_s, *rest = refs
    low, last_h = rest[:4], rest[4:]
    r = Round(rounds, lat, prior, from_a, w_in, w_mid, low, lambda g, p: kept_h.at[g] if p == 2 else last_h[g], lambda g, p: kept_s.at[g])
    rows = list(range(4, 10))
    units = len(r.groups)
    for g in range(units + 1):
        if g < units:
            r.fill(g, rows)
            r.hidden_pair(g, 2, 4)
            r.hidden_pair(g, 3, 4)
        if g:
            r.second_pair(g - 1, 2)


def second_part(rounds, *refs):
    lat, from_b = refs[:2]
    prior = refs[2] if rounds else None
    kept_h, kept_s, w_in, w_mid, w_out, steps, *rest = refs[3 if rounds else 2:]
    last = rounds == 2
    if last:
        out, rest = rest[:4], rest[4:]
        ready = rest.pop()
    else:
        nxt, to_a, to_b, *rest = rest
    low, hid, sec = rest[:4], rest[4:12], rest[12:20]
    r = Round(rounds, lat, prior, from_b, w_in, w_mid, low, lambda g, p: hid[g * 2 + p] if p < 2 else kept_h.at[g], lambda g, p: sec[g * 2 + p] if p < 2 else kept_s.at[g])
    core, tm, column = r.core, r.tm, r.column

    def keep(t, row, value):
        ready[pl.ds(((t // 2) ^ tm) * 128 + (t % 2) * 64 + row + core * (3 - 2 * row), C, stride=ROWS), :] = value

    totals = [jnp.zeros((C, L), F32) if rounds == 0 else prior[0, row] for row in range(ROWS)]

    def out_pair(g, p):
        t0, n = r.groups[g]
        width = n * L
        rhs = jnp.concatenate([r.sec(g, p)[:, :width], r.sec(g, p + 1)[:, :width]], axis=0)
        y = jnp.dot(w_out[...], rhs, preferred_element_type=F32)
        for q in range(2):
            row = 2 * p + q
            for i in range(n):
                t = t0 + i
                part = y[q * 48:(q + 1) * 48, i * L:(i + 1) * L]
                conv = pltpu.roll(part[:C] * column, 1, 1) + part[C:2 * C] + pltpu.roll(part[2 * C:] * column, L - 1, 1)
                totals[row] = totals[row] + steps[t:t + 1] * (r.state(t, row) + conv)
                value = lat[row] + totals[row]
                if last:
                    keep(t, row, value)
                else:
                    nxt[t + 1, row] = value
                    if t == rounds:
                        nxt[0, row] = totals[row]
                    if t < TIMES - 1 and row < 3:
                        to_b[t - rounds, row] = value.astype(BF)
                    if t < TIMES - 1 and row > 0:
                        to_a[t - rounds, 3 - row] = value.astype(BF)

    rows = list(range(6))
    units = len(r.groups)
    for g in range(units + 2):
        if g < units:
            r.fill(g, rows)
            r.hidden_pair(g, 1, 0)
            r.hidden_pair(g, 0, 0)
        if 0 < g <= units:
            r.second_pair(g - 1, 1)
            r.second_pair(g - 1, 0)
        if g > 1:
            out_pair(g - 2, 1)
            out_pair(g - 2, 0)

    for row in range(ROWS):
        if rounds == 1:
            nxt[1, row] = prior[1, row]
        if last:
            for t in range(2):
                keep(t, row, prior[t + 1, row])
    if last:
        for k in range(4):
            out[k][...] = ready[k * 128:(k + 1) * 128].reshape(32, ROWS, L)


def call(body, rounds, args, out_shape, scratch):
    return pl.pallas_call(
        functools.partial(body, rounds),
        out_shape=out_shape,
        in_specs=[VM] * len(args),
        out_specs=(VM,) * len(out_shape),
        scratch_shapes=scratch,
        compiler_params=pltpu.CompilerParams(vmem_limit_bytes=24 << 20),
    )(*args)


PAIR = (2 * F, 2 * L)
LOW = [pltpu.VMEM((288, 2 * L), BF)] * 4


def run_first(rounds, *args):
    out_shape = (jax.ShapeDtypeStruct((len(groups_of(rounds)),) + PAIR, BF),) * 2
    scratch = LOW + [pltpu.VMEM(PAIR, BF)] * 4
    if rounds == 0:
        out_shape += (jax.ShapeDtypeStruct((3 * F, 2 * F), BF), jax.ShapeDtypeStruct((TIMES, F), F32))
        scratch += [pltpu.VMEM((4, 16, F), F32)]
    return call(first_part, rounds, args, out_shape, scratch)


def run_second(rounds, *args):
    scratch = LOW + [pltpu.VMEM(PAIR, BF)] * 16
    if rounds == 2:
        out_shape = (jax.ShapeDtypeStruct((32, ROWS, L), F32),) * 4
        scratch += [pltpu.VMEM((512, L), F32)]
    else:
        sent = jax.ShapeDtypeStruct((TIMES - 1 - rounds, 3, C, L), BF)
        out_shape = (jax.ShapeDtypeStruct((TIMES + 1, ROWS, C, L), F32), sent, sent)
    return call(second_part, rounds, args, out_shape, scratch)


def join_body(p0, p1, p2, p3, out):
    tm = lax.axis_index("tm")
    pieces = [p0[...], p1[...], p2[...], p3[...]]
    lane = lax.broadcasted_iota(jnp.int32, pieces[0].shape, 2)
    placed = []
    for t in range(4):
        x = by_tm(t ^ tm, pieces)
        placed.append(pltpu.roll(x, STARTS[t] % L, 2))
    for g in range(3):
        out[:, :, g * L:(g + 1) * L] = jnp.where(lane < CUTS[g] - g * L, placed[g], placed[g + 1])
    out[:, :, 3 * L:] = placed[3][:, :, :448 - 3 * L]


def join(pieces):
    return pl.pallas_call(
        join_body,
        out_shape=jax.ShapeDtypeStruct((32, ROWS, 448), F32),
        in_specs=[VM] * 4,
        out_specs=VM,
        compiler_params=pltpu.CompilerParams(vmem_limit_bytes=8 << 20),
        name="join",
    )(*pieces)


def across(x, k):
    return lax.ppermute(x, "tm", [(t, t ^ k) for t in range(4)])


def pair_up(x, pairs):
    return lax.ppermute(x, "pix", [(a, b) for a, b in pairs] + [(b, a) for a, b in pairs])


def partner_of_other_half(x):
    pixels = lax.axis_size("pix")
    pairs = [(t * pixels + p, (t ^ 2) * pixels + (p ^ 1)) for t in range(4) for p in range(pixels)]
    return lax.ppermute(x, ("tm", "pix"), pairs)


CORES = [(2 * k, 2 * k + 1) for k in range(32)]
CHIPS = [(2 * k + 1, 2 * k + 2) for k in range(31)]


def shards(latent, step_size, time_embed, conv_in, conv_mid, conv_out):
    lat, to_a, to_b, small = enter(step_size, latent, time_embed)
    smalls = [small]
    for k in (1, 3):
        smalls.append(across(small, k))
    w_conv, w_mid, w_out = prepare(conv_in.transpose(0, 1, 3, 2), conv_mid, conv_out)
    prior = ()
    for rounds in range(3):
        from_b = pair_up(to_b, CHIPS)
        from_a = pair_up(to_a, CORES) if rounds else partner_of_other_half(to_a)
        if rounds == 0:
            *kept, w_in, steps = run_first(0, lat, from_a, *smalls, w_conv, w_mid)
        else:
            kept = run_first(rounds, lat, from_a, *prior, w_in, w_mid)
        done = run_second(rounds, lat, from_b, *prior, *kept, w_in, w_mid, w_out, steps)
        if rounds < 2:
            *prior, to_a, to_b = done
    got = [done[0]]
    for k in (1, 2, 3):
        got.append(across(done[k], k))
    return join(got).reshape(2, C, ROWS, 448)


def solution(mesh):
    in_specs = (P(None, "pix", None), P("tm"), P("tm", None), P(), P(), P())
    out_specs = P("tm", None, "pix", None)
    return jax.shard_map(shards, mesh=mesh, in_specs=in_specs, out_specs=out_specs, check_vma=False)
```

```python
import functools

import jax
import jax.numpy as jnp
from jax import lax
from jax.experimental import pallas as pl
from jax.experimental.pallas import tpu as pltpu
from jax.sharding import PartitionSpec as P


TIMES = 8
C = 16
F = 128
L = 128
ROWS = 4
STARTS = (-1, 105, 215, 321)
SHIFTS = tuple(-start % L for start in STARTS)
CUTS = (114, 224, 334)
BF = jnp.bfloat16
F32 = jnp.float32


VM = pl.BlockSpec(memory_space=pltpu.VMEM)
ANY = pl.BlockSpec(memory_space=pltpu.HBM)


def by_tm(tm, values):
    return jnp.where(tm == 0, values[0], jnp.where(tm == 1, values[1], jnp.where(tm == 2, values[2], values[3])))


def pieces_of(x):
    high = x.astype(BF).astype(F32)
    rest = x - high
    middle = rest.astype(BF).astype(F32)
    return high, middle, rest - middle


def enter_body(step, latent, embed, lat, to_a, to_b, small, step_s, latent_v, embed_v, other, sems):
    copies = [pltpu.make_async_copy(x, y, sems.at[i]) for i, (x, y) in enumerate(((latent, latent_v), (embed, embed_v), (step, step_s)))]
    for copy in copies:
        copy.start()
    for copy in copies:
        copy.wait()
    tm, core = lax.axis_index("tm"), lax.axis_index("pix") % 2
    lane = lax.broadcasted_iota(jnp.int32, (C, L), 1)
    for r in range(ROWS):
        tiles = [jnp.zeros((C, L), F32)] + [latent_v[:, r, g * L:(g + 1) * L] for g in range(3)]
        tiles.append(jnp.concatenate([latent_v[:, r, 3 * L:], jnp.zeros((C, 4 * L - 448), F32)], axis=1))
        for t, to in ((tm, lat), (tm ^ 2, other)):
            shift = by_tm(t, SHIFTS)
            left, right = by_tm(t, tiles[:4]), by_tm(t, tiles[1:])
            to[r + core * (3 - 2 * r)] = jnp.where(lane < shift, pltpu.roll(left, shift, 1), pltpu.roll(right, shift, 1))
    for d in range(3):
        to_b[d] = lat[d].astype(BF)
        to_a[d] = other[3 - d].astype(BF)
    rows = jnp.concatenate([embed_v[...]] + [jnp.full((1, F), step_s[d], F32) for d in range(2)], axis=0)
    table = jnp.concatenate([*pieces_of(rows), jnp.zeros((4, F), F32)], axis=0).astype(BF)
    small[...] = table
    to_a[3] = table


def enter(step, latent, embed):
    shapes = ((4, C, L), (3, C, L), (16, F))
    return pl.pallas_call(
        enter_body,
        out_shape=(jax.ShapeDtypeStruct((ROWS, C, L), F32),) + tuple(jax.ShapeDtypeStruct(shape, BF) for shape in shapes),
        in_specs=[ANY] * 3,
        out_specs=(VM,) * 4,
        scratch_shapes=[
            pltpu.SMEM((2,), F32),
            pltpu.VMEM((C, ROWS, 448), F32),
            pltpu.VMEM((2, F), F32),
            pltpu.VMEM((ROWS, C, L), F32),
            pltpu.SemaphoreType.DMA((3,)),
        ],
        compiler_params=pltpu.CompilerParams(vmem_limit_bytes=4 << 20),
        name="enter",
    )(*[pltpu.with_memory_space_constraint(v, pltpu.HBM) for v in (step, latent, embed)])


def prepare_body(conv_in, conv_mid, conv_out, w_in, w_mid, w_out, in_v, mid_v, out_v, turned, sems):
    copies = [pltpu.make_async_copy(x, y, sems.at[i]) for i, (x, y) in enumerate(((conv_in, in_v), (conv_mid, mid_v), (conv_out, out_v)))]
    for copy in copies:
        copy.start()
    core = lax.axis_index("pix") % 2
    w_mid[...] = jnp.zeros_like(w_mid)
    w_out[...] = jnp.zeros_like(w_out)
    turned[...] = jnp.zeros_like(turned)
    for copy in copies:
        copy.wait()
    for a in range(3):
        row = a + core * (2 - 2 * a)
        for b in range(3):
            mid = mid_v[row, b] * 0.5
            tail = out_v[row, b]
            head = in_v[row, b] * 0.5
            for q in range(2):
                w_mid[(b * 2 + q) * F:(b * 2 + q + 1) * F, (a + q) * F:(a + q + 1) * F] = mid
                w_out[q * 48 + b * C:q * 48 + (b + 1) * C, (a + q) * F:(a + q + 1) * F] = tail
                turned[(a + q) * 48 + b * C:(a + q) * 48 + (b + 1) * C, q * F:(q + 1) * F] = head
    w_in[:2 * F] = turned[...].astype(F32).T.astype(BF)
    w_in[2 * F:] = jnp.zeros((F, 2 * F), BF)


def prepare(conv_in, conv_mid, conv_out):
    shapes = ((3 * F, 2 * F), (7 * F, 4 * F), (96, 4 * F))
    return pl.pallas_call(
        prepare_body,
        out_shape=tuple(jax.ShapeDtypeStruct(shape, BF) for shape in shapes),
        in_specs=[ANY] * 3,
        out_specs=(VM,) * 3,
        scratch_shapes=[
            pltpu.VMEM((3, 3, C, F), BF),
            pltpu.VMEM((3, 3, F, F), BF),
            pltpu.VMEM((3, 3, C, F), BF),
            pltpu.VMEM((2 * F, 2 * F), BF),
            pltpu.SemaphoreType.DMA((3,)),
        ],
        compiler_params=pltpu.CompilerParams(vmem_limit_bytes=8 << 20),
        name="prepare",
    )(*[pltpu.with_memory_space_constraint(v, pltpu.HBM) for v in (conv_in, conv_mid, conv_out)])


def tables(tm, smalls, w_conv, w_in, steps, gathered):
    for k in range(4):
        gathered[tm ^ k] = smalls[k].astype(F32)
    high, middle, rest = [jnp.concatenate([gathered[t, at:at + 2] for t in range(4)], axis=0) * 0.5 for at in (0, 4, 8)]
    steps[...] = sum(jnp.concatenate([gathered[t, at:at + 2] for t in range(4)], axis=0) for at in (2, 6, 10))
    tail = jnp.concatenate([jnp.zeros((64, F), F32), high, middle, rest, jnp.zeros((40, F), F32)], axis=0)
    tail = tail.T.astype(BF)
    w_in[:, :F] = w_conv[:, :F]
    for q in range(2):
        w_in[q * F:(q + 1) * F, F:] = w_conv[q * F:(q + 1) * F, F:] + tail
    w_in[2 * F:, F:] = w_conv[2 * F:, F:]


def silu2(v):
    return v + v * jnp.tanh(v)


def groups_of(rounds):
    return [(t0, min(2, TIMES - t0)) for t0 in range(rounds, TIMES, 2)]


class Round:
    def __init__(self, rounds, lat, prior, halo, w_in, w_mid, w_out, steps, low, first_row):
        self.rounds, self.lat, self.prior, self.halo = rounds, lat, prior, halo
        self.w_in, self.w_mid, self.w_out, self.steps = w_in, w_mid, w_out, steps
        self.low, self.first_row = low, first_row
        pix, self.tm = lax.axis_index("pix"), lax.axis_index("tm")
        self.core = pix % 2
        self.inside = (pix > 0) & (pix < 63)
        self.groups = groups_of(rounds)
        lane = lax.broadcasted_iota(jnp.int32, (C, L), 1)
        self.column = jnp.where(((self.tm == 0) & (lane == 0)) | ((self.tm == 3) & (lane == L - 1)), 0.0, 1.0)
        self.totals = {}

    def state(self, t, row):
        return self.lat[row] if self.rounds == 0 else self.prior[t, row]

    def fill(self, g, rows):
        t0, n = self.groups[g]
        rounds, column = self.rounds, self.column
        for w in rows:
            for i in range(n if rounds else 1):
                if 3 <= w < 7:
                    x = self.state(t0 + i, w - 3)
                else:
                    d = 2 - w if w < 3 else w - 7
                    x = self.halo[(t0 + i - rounds, d) if rounds else (d,)].astype(F32)
                x = x * column
                x = jnp.concatenate([pltpu.roll(x, 1, 1) * column, x, pltpu.roll(x, L - 1, 1) * column], axis=0).astype(BF)
                at = (w - self.first_row) * 48
                for lanes in ([i] if rounds else range(n)):
                    self.low[g][at:at + 48, lanes * L:(lanes + 1) * L] = x

    def block(self, row, last, normal, zero):
        return normal * F if row > last else pl.multiple_of(jnp.where(self.inside, normal * F, zero * F), F)

    def hidden(self, g, row, to):
        t0, n = self.groups[g]
        width = n * L
        r = lax.broadcasted_iota(jnp.int32, (64, width), 0)
        c = lax.broadcasted_iota(jnp.int32, (64, width), 1)
        edge = ((self.tm == 0) & ((c & 127) == 0)) | ((self.tm == 3) & ((c & 127) == L - 1))
        pick = jnp.where(((r & 7) == t0 + (c >> 7)) & (r < 24) & jnp.logical_not(edge), 1.0, 0.0).astype(BF)
        at = (row - 1 - self.first_row) * 48
        rhs = jnp.concatenate([self.low[g][at:at + 192, :width], pick], axis=0)
        blocks = [self.w_in[pl.ds(self.block(row + q, 2, q, 2), F), :] for q in range(len(to))]
        v = silu2(jnp.dot(jnp.concatenate(blocks, axis=0), rhs, preferred_element_type=F32)).astype(BF)
        for q, (ref, place) in enumerate(to):
            ref[place * F:(place + 1) * F, :width] = v[q * F:(q + 1) * F]

    def second(self, g, row, sources, to):
        _, n = self.groups[g]
        count = len(to)
        rhs = jnp.concatenate([ref[at * F:(at + k) * F, :n * L] for ref, at, k in sources], axis=0)
        depth = (count + 2) * F
        blocks = [self.w_mid[pl.ds(self.block(row + q, 2, 2 * b + q, 6), F), :depth] for b in range(3) for q in range(count)]
        y = jnp.dot(jnp.concatenate(blocks, axis=0), rhs, preferred_element_type=F32)
        m = count * F
        for i in range(n):
            lanes = slice(i * L, (i + 1) * L)
            part = y[:, lanes]
            v = pltpu.roll(part[:m], 1, 1) + part[m:2 * m] + pltpu.roll(part[2 * m:], L - 1, 1)
            v = silu2(v).astype(BF)
            for q, (ref, place) in enumerate(to):
                ref[place * F:(place + 1) * F, lanes] = v[q * F:(q + 1) * F]

    def output(self, g, row, count, sources, emit):
        t0, n = self.groups[g]
        column = self.column
        rhs = jnp.concatenate([ref[at * F:(at + k) * F, :n * L] for ref, at, k in sources], axis=0)
        y = jnp.dot(self.w_out[:count * 48, :(count + 2) * F], rhs, preferred_element_type=F32)
        for q in range(count):
            own = row + q
            if own not in self.totals:
                self.totals[own] = jnp.zeros((C, L), F32) if self.rounds == 0 else self.prior[0, own]
            for i in range(n):
                t = t0 + i
                part = y[q * 48:(q + 1) * 48, i * L:(i + 1) * L]
                conv = pltpu.roll(part[:C] * column, 1, 1) + part[C:2 * C] + pltpu.roll(part[2 * C:] * column, L - 1, 1)
                self.totals[own] = self.totals[own] + self.steps[t:t + 1] * (self.state(t, own) + conv)
                emit(t, own, self.lat[own] + self.totals[own], self.totals[own])


def first_part(rounds, *refs):
    if rounds == 0:
        lat, from_a, own, one, three, w_conv, w_mid, w_out, kept_h, kept_s, done, w_in, steps, *rest = refs
        smalls = [own[...], one[...], from_a[3], three[...]]
        tables(lax.axis_index("tm"), smalls, w_conv, w_in, steps, rest.pop())
        prior = None
    else:
        lat, from_a, prior, w_in, steps, w_mid, w_out, kept_h, kept_s, done, *rest = refs
    low, hid, sec = rest[:4], rest[4:8], rest[8:12]
    r = Round(rounds, lat, prior, from_a, w_in, w_mid, w_out, steps, low, 3)

    def emit(t, row, value, total):
        done[t + 1] = value
        if t == rounds:
            done[0] = total

    units = len(r.groups)
    for g in range(units + 2):
        if g < units:
            r.fill(g, list(range(3, 10)))
            r.hidden(g, 5, [(kept_h.at[g], 1), (hid[g], 0)])
            r.hidden(g, 7, [(hid[g], 1), (hid[g], 2)])
            r.hidden(g, 4, [(kept_h.at[g], 0)])
        if 0 < g <= units:
            k = g - 1
            r.second(k, 6, [(kept_h.at[k], 1, 1), (hid[k], 0, 3)], [(kept_s.at[k], 1), (sec[k], 0)])
            r.second(k, 5, [(kept_h.at[k], 0, 2), (hid[k], 0, 1)], [(kept_s.at[k], 0)])
        if g > 1:
            k = g - 2
            r.output(k, 3, 1, [(kept_s.at[k], 0, 2), (sec[k], 0, 1)], emit)


def second_part(rounds, *refs):
    lat, from_b = refs[:2]
    prior = refs[2] if rounds else None
    kept_h, kept_s, done, w_in, w_mid, w_out, steps, *rest = refs[3 if rounds else 2:]
    last = rounds == 2
    if last:
        out, rest = rest[:4], rest[4:]
        ready = rest.pop()
    else:
        nxt, to_a, to_b, *rest = rest
    low, hid, sec = rest[:4], rest[4:8], rest[8:12]
    r = Round(rounds, lat, prior, from_b, w_in, w_mid, w_out, steps, low, 0)
    core, tm = r.core, r.tm

    def keep(t, row, value):
        ready[pl.ds(((t // 2) ^ tm) * 128 + (t % 2) * 64 + row + core * (3 - 2 * row), C, stride=ROWS), :] = value

    def emit(t, row, value, total):
        if last:
            keep(t, row, value)
            return
        nxt[t + 1, row] = value
        if t == rounds:
            nxt[0, row] = total
        if t < TIMES - 1 and row < 3:
            to_b[t - rounds, row] = value.astype(BF)
        if t < TIMES - 1 and row > 0:
            to_a[t - rounds, 3 - row] = value.astype(BF)

    units = len(r.groups)
    for g in range(units + 2):
        if g < units:
            r.fill(g, list(range(6)))
            r.hidden(g, 2, [(hid[g], 1), (hid[g], 2)])
            r.hidden(g, 1, [(hid[g], 0)])
        if 0 < g <= units:
            k = g - 1
            r.second(k, 2, [(hid[k], 0, 3), (kept_h.at[k], 0, 1)], [(sec[k], 0), (sec[k], 1)])
            r.second(k, 4, [(hid[k], 2, 1), (kept_h.at[k], 0, 2)], [(sec[k], 2)])
        if g > 1:
            k = g - 2
            r.output(k, 0, 2, [(sec[k], 0, 3), (kept_s.at[k], 0, 1)], emit)
            r.output(k, 2, 1, [(sec[k], 2, 1), (kept_s.at[k], 0, 2)], emit)

    for t in range(rounds, TIMES):
        emit(t, 3, done[t + 1], done[0])
    for row in range(ROWS):
        if rounds == 1:
            nxt[1, row] = prior[1, row]
        if last:
            for t in range(2):
                keep(t, row, prior[t + 1, row])
    if last:
        for k in range(4):
            out[k][...] = ready[k * 128:(k + 1) * 128].reshape(32, ROWS, L)


def call(body, rounds, args, out_shape, scratch):
    return pl.pallas_call(
        functools.partial(body, rounds),
        out_shape=out_shape,
        in_specs=[VM] * len(args),
        out_specs=(VM,) * len(out_shape),
        scratch_shapes=scratch,
        compiler_params=pltpu.CompilerParams(vmem_limit_bytes=24 << 20),
    )(*args)


PAIR = (2 * F, 2 * L)


def scratch_of(low_rows, sec_rows):
    shapes = ((low_rows * 48, 2 * L), (3 * F, 2 * L), (sec_rows * F, 2 * L))
    return [pltpu.VMEM(shape, BF) for shape in shapes for _ in range(4)]


def run_first(rounds, *args):
    units = len(groups_of(rounds))
    out_shape = (jax.ShapeDtypeStruct((units,) + PAIR, BF),) * 2 + (jax.ShapeDtypeStruct((TIMES + 1, C, L), F32),)
    scratch = scratch_of(7, 1)
    if rounds == 0:
        out_shape += (jax.ShapeDtypeStruct((3 * F, 2 * F), BF), jax.ShapeDtypeStruct((TIMES, F), F32))
        scratch += [pltpu.VMEM((4, 16, F), F32)]
    return call(first_part, rounds, args, out_shape, scratch)


def run_second(rounds, *args):
    scratch = scratch_of(6, 3)
    if rounds == 2:
        out_shape = (jax.ShapeDtypeStruct((32, ROWS, L), F32),) * 4
        scratch += [pltpu.VMEM((512, L), F32)]
    else:
        sent = jax.ShapeDtypeStruct((TIMES - 1 - rounds, 3, C, L), BF)
        out_shape = (jax.ShapeDtypeStruct((TIMES + 1, ROWS, C, L), F32), sent, sent)
    return call(second_part, rounds, args, out_shape, scratch)


def join_body(p0, p1, p2, p3, out):
    tm = lax.axis_index("tm")
    pieces = [p0[...], p1[...], p2[...], p3[...]]
    lane = lax.broadcasted_iota(jnp.int32, pieces[0].shape, 2)
    placed = []
    for t in range(4):
        x = by_tm(t ^ tm, pieces)
        placed.append(pltpu.roll(x, STARTS[t] % L, 2))
    for g in range(3):
        out[:, :, g * L:(g + 1) * L] = jnp.where(lane < CUTS[g] - g * L, placed[g], placed[g + 1])
    out[:, :, 3 * L:] = placed[3][:, :, :448 - 3 * L]


def join(pieces):
    return pl.pallas_call(
        join_body,
        out_shape=jax.ShapeDtypeStruct((32, ROWS, 448), F32),
        in_specs=[VM] * 4,
        out_specs=VM,
        compiler_params=pltpu.CompilerParams(vmem_limit_bytes=8 << 20),
        name="join",
    )(*pieces)


def across(x, k):
    return lax.ppermute(x, "tm", [(t, t ^ k) for t in range(4)])


def pair_up(x, pairs):
    return lax.ppermute(x, "pix", [(a, b) for a, b in pairs] + [(b, a) for a, b in pairs])


def partner_of_other_half(x):
    pixels = lax.axis_size("pix")
    pairs = [(t * pixels + p, (t ^ 2) * pixels + (p ^ 1)) for t in range(4) for p in range(pixels)]
    return lax.ppermute(x, ("tm", "pix"), pairs)


CORES = [(2 * k, 2 * k + 1) for k in range(32)]
CHIPS = [(2 * k + 1, 2 * k + 2) for k in range(31)]


def shards(latent, step_size, time_embed, conv_in, conv_mid, conv_out):
    lat, to_a, to_b, small = enter(step_size, latent, time_embed)
    smalls = [small]
    for k in (1, 3):
        smalls.append(across(small, k))
    w_conv, w_mid, w_out = prepare(conv_in.transpose(0, 1, 3, 2), conv_mid, conv_out)
    prior = ()
    for rounds in range(3):
        from_b = pair_up(to_b, CHIPS)
        from_a = pair_up(to_a, CORES) if rounds else partner_of_other_half(to_a)
        if rounds == 0:
            *kept, w_in, steps = run_first(0, lat, from_a, *smalls, w_conv, w_mid, w_out)
        else:
            kept = run_first(rounds, lat, from_a, *prior, w_in, steps, w_mid, w_out)
        done = run_second(rounds, lat, from_b, *prior, *kept, w_in, w_mid, w_out, steps)
        if rounds < 2:
            *prior, to_a, to_b = done
    got = [done[0]]
    for k in (1, 2, 3):
        got.append(across(done[k], k))
    return join(got).reshape(2, C, ROWS, 448)


def solution(mesh):
    in_specs = (P(None, "pix", None), P("tm"), P("tm", None), P(), P(), P())
    out_specs = P("tm", None, "pix", None)
    return jax.shard_map(shards, mesh=mesh, in_specs=in_specs, out_specs=out_specs, check_vma=False)
```

```python
import functools

import jax
import jax.numpy as jnp
from jax import lax
from jax.experimental import pallas as pl
from jax.experimental.pallas import tpu as pltpu
from jax.sharding import PartitionSpec as P


TIMES = 8
C = 16
F = 128
L = 128
ROWS = 4
STARTS = (-1, 105, 215, 321)
SHIFTS = tuple(-start % L for start in STARTS)
CUTS = (114, 224, 334)
BF = jnp.bfloat16
F32 = jnp.float32


VM = pl.BlockSpec(memory_space=pltpu.VMEM)
ANY = pl.BlockSpec(memory_space=pltpu.HBM)


def by_tm(tm, values):
    return jnp.where(tm == 0, values[0], jnp.where(tm == 1, values[1], jnp.where(tm == 2, values[2], values[3])))


def pieces_of(x):
    high = x.astype(BF).astype(F32)
    rest = x - high
    middle = rest.astype(BF).astype(F32)
    return high, middle, rest - middle


def enter_body(step, latent, embed, lat, to_a, to_b, small, step_s, latent_v, embed_v, other, sems):
    copies = [pltpu.make_async_copy(x, y, sems.at[i]) for i, (x, y) in enumerate(((latent, latent_v), (embed, embed_v), (step, step_s)))]
    for copy in copies:
        copy.start()
    for copy in copies:
        copy.wait()
    tm, core = lax.axis_index("tm"), lax.axis_index("pix") % 2
    lane = lax.broadcasted_iota(jnp.int32, (C, L), 1)
    for r in range(ROWS):
        tiles = [jnp.zeros((C, L), F32)] + [latent_v[:, r, g * L:(g + 1) * L] for g in range(3)]
        tiles.append(jnp.concatenate([latent_v[:, r, 3 * L:], jnp.zeros((C, 4 * L - 448), F32)], axis=1))
        for t, to in ((tm, lat), (tm ^ 2, other)):
            shift = by_tm(t, SHIFTS)
            left, right = by_tm(t, tiles[:4]), by_tm(t, tiles[1:])
            to[r + core * (3 - 2 * r)] = jnp.where(lane < shift, pltpu.roll(left, shift, 1), pltpu.roll(right, shift, 1))
    for d in range(3):
        to_b[d] = lat[d].astype(BF)
        to_a[d] = other[3 - d].astype(BF)
    rows = jnp.concatenate([embed_v[...]] + [jnp.full((1, F), step_s[d], F32) for d in range(2)], axis=0)
    table = jnp.concatenate([*pieces_of(rows), jnp.zeros((4, F), F32)], axis=0).astype(BF)
    small[...] = table
    to_a[3] = table


def enter(step, latent, embed):
    shapes = ((4, C, L), (3, C, L), (16, F))
    return pl.pallas_call(
        enter_body,
        out_shape=(jax.ShapeDtypeStruct((ROWS, C, L), F32),) + tuple(jax.ShapeDtypeStruct(shape, BF) for shape in shapes),
        in_specs=[ANY] * 3,
        out_specs=(VM,) * 4,
        scratch_shapes=[
            pltpu.SMEM((2,), F32),
            pltpu.VMEM((C, ROWS, 448), F32),
            pltpu.VMEM((2, F), F32),
            pltpu.VMEM((ROWS, C, L), F32),
            pltpu.SemaphoreType.DMA((3,)),
        ],
        compiler_params=pltpu.CompilerParams(vmem_limit_bytes=4 << 20),
        name="enter",
    )(*[pltpu.with_memory_space_constraint(v, pltpu.HBM) for v in (step, latent, embed)])


def prepare_body(conv_in, conv_mid, conv_out, w_in, w_mid, w_out, in_v, mid_v, out_v, turned, sems):
    copies = [pltpu.make_async_copy(x, y, sems.at[i]) for i, (x, y) in enumerate(((conv_in, in_v), (conv_mid, mid_v), (conv_out, out_v)))]
    for copy in copies:
        copy.start()
    core = lax.axis_index("pix") % 2
    w_mid[...] = jnp.zeros_like(w_mid)
    w_out[...] = jnp.zeros_like(w_out)
    turned[...] = jnp.zeros_like(turned)
    for copy in copies:
        copy.wait()
    for a in range(3):
        row = a + core * (2 - 2 * a)
        for b in range(3):
            mid = mid_v[row, b] * 0.5
            tail = out_v[row, b]
            head = in_v[row, b] * 0.5
            for q in range(2):
                w_mid[(b * 2 + q) * F:(b * 2 + q + 1) * F, (a + q) * F:(a + q + 1) * F] = mid
                w_out[q * 48 + b * C:q * 48 + (b + 1) * C, (a + q) * F:(a + q + 1) * F] = tail
                turned[(a + q) * 48 + b * C:(a + q) * 48 + (b + 1) * C, q * F:(q + 1) * F] = head
    w_in[:2 * F] = turned[...].astype(F32).T.astype(BF)
    w_in[2 * F:] = jnp.zeros((F, 2 * F), BF)


def prepare(conv_in, conv_mid, conv_out):
    shapes = ((3 * F, 2 * F), (7 * F, 4 * F), (96, 4 * F))
    return pl.pallas_call(
        prepare_body,
        out_shape=tuple(jax.ShapeDtypeStruct(shape, BF) for shape in shapes),
        in_specs=[ANY] * 3,
        out_specs=(VM,) * 3,
        scratch_shapes=[
            pltpu.VMEM((3, 3, C, F), BF),
            pltpu.VMEM((3, 3, F, F), BF),
            pltpu.VMEM((3, 3, C, F), BF),
            pltpu.VMEM((2 * F, 2 * F), BF),
            pltpu.SemaphoreType.DMA((3,)),
        ],
        compiler_params=pltpu.CompilerParams(vmem_limit_bytes=8 << 20),
        name="prepare",
    )(*[pltpu.with_memory_space_constraint(v, pltpu.HBM) for v in (conv_in, conv_mid, conv_out)])


def tables(tm, smalls, w_conv, w_in, steps, gathered):
    for k, small in smalls:
        gathered[tm ^ k] = small.astype(F32)
    high, middle, rest = [jnp.concatenate([gathered[t, at:at + 2] for t in range(4)], axis=0) * 0.5 for at in (0, 4, 8)]
    steps[...] = sum(jnp.concatenate([gathered[t, at:at + 2] for t in range(4)], axis=0) for at in (2, 6, 10))
    tail = jnp.concatenate([jnp.zeros((64, F), F32), high, middle, rest, jnp.zeros((40, F), F32)], axis=0)
    tail = tail.T.astype(BF)
    w_in[:, :F] = w_conv[:, :F]
    for q in range(2):
        w_in[q * F:(q + 1) * F, F:] = w_conv[q * F:(q + 1) * F, F:] + tail
    w_in[2 * F:, F:] = w_conv[2 * F:, F:]


def silu2(v):
    return v + v * jnp.tanh(v)


def groups_of(rounds):
    return [(t0, min(2, TIMES - t0)) for t0 in range(rounds, TIMES, 2)]


class Round:
    def __init__(self, rounds, lat, prior, halo, w_in, w_mid, w_out, steps, low, first_row):
        self.rounds, self.lat, self.prior, self.halo = rounds, lat, prior, halo
        self.w_in, self.w_mid, self.w_out, self.steps = w_in, w_mid, w_out, steps
        self.low, self.first_row = low, first_row
        pix, self.tm = lax.axis_index("pix"), lax.axis_index("tm")
        self.core = pix % 2
        self.inside = (pix > 0) & (pix < 63)
        self.groups = groups_of(rounds)
        lane = lax.broadcasted_iota(jnp.int32, (C, L), 1)
        self.column = jnp.where(((self.tm == 0) & (lane == 0)) | ((self.tm == 3) & (lane == L - 1)), 0.0, 1.0)
        self.totals = {}

    def state(self, t, row):
        return self.lat[row] if self.rounds == 0 else self.prior[t, row]

    def fill(self, g, rows):
        t0, n = self.groups[g]
        rounds, column = self.rounds, self.column
        for w in rows:
            for i in range(n if rounds else 1):
                if 3 <= w < 7:
                    x = self.state(t0 + i, w - 3)
                else:
                    d = 2 - w if w < 3 else w - 7
                    x = self.halo[(t0 + i - rounds, d) if rounds else (d,)].astype(F32)
                x = x * column
                x = jnp.concatenate([pltpu.roll(x, 1, 1) * column, x, pltpu.roll(x, L - 1, 1) * column], axis=0).astype(BF)
                at = (w - self.first_row) * 48
                for lanes in ([i] if rounds else range(n)):
                    self.low[g][at:at + 48, lanes * L:(lanes + 1) * L] = x

    def block(self, row, last, normal, zero):
        return normal * F if row > last else pl.multiple_of(jnp.where(self.inside, normal * F, zero * F), F)

    def hidden(self, g, row, to):
        t0, n = self.groups[g]
        width = n * L
        r = lax.broadcasted_iota(jnp.int32, (64, width), 0)
        c = lax.broadcasted_iota(jnp.int32, (64, width), 1)
        edge = ((self.tm == 0) & ((c & 127) == 0)) | ((self.tm == 3) & ((c & 127) == L - 1))
        pick = jnp.where(((r & 7) == t0 + (c >> 7)) & (r < 24) & jnp.logical_not(edge), 1.0, 0.0).astype(BF)
        at = (row - 1 - self.first_row) * 48
        rhs = jnp.concatenate([self.low[g][at:at + 192, :width], pick], axis=0)
        blocks = [self.w_in[pl.ds(self.block(row + q, 2, q, 2), F), :] for q in range(len(to))]
        v = silu2(jnp.dot(jnp.concatenate(blocks, axis=0), rhs, preferred_element_type=F32)).astype(BF)
        for q, (ref, place) in enumerate(to):
            ref[place * F:(place + 1) * F, :width] = v[q * F:(q + 1) * F]

    def second(self, g, row, sources, to):
        _, n = self.groups[g]
        count = len(to)
        rhs = jnp.concatenate([ref[at * F:(at + k) * F, :n * L] for ref, at, k in sources], axis=0)
        depth = (count + 2) * F
        blocks = [self.w_mid[pl.ds(self.block(row + q, 2, 2 * b + q, 6), F), :depth] for b in range(3) for q in range(count)]
        y = jnp.dot(jnp.concatenate(blocks, axis=0), rhs, preferred_element_type=F32)
        m = count * F
        for i in range(n):
            lanes = slice(i * L, (i + 1) * L)
            part = y[:, lanes]
            v = pltpu.roll(part[:m], 1, 1) + part[m:2 * m] + pltpu.roll(part[2 * m:], L - 1, 1)
            v = silu2(v).astype(BF)
            for q, (ref, place) in enumerate(to):
                ref[place * F:(place + 1) * F, lanes] = v[q * F:(q + 1) * F]

    def output(self, g, row, count, sources, emit):
        t0, n = self.groups[g]
        column = self.column
        rhs = jnp.concatenate([ref[at * F:(at + k) * F, :n * L] for ref, at, k in sources], axis=0)
        y = jnp.dot(self.w_out[:count * 48, :(count + 2) * F], rhs, preferred_element_type=F32)
        for q in range(count):
            own = row + q
            if own not in self.totals:
                self.totals[own] = jnp.zeros((C, L), F32) if self.rounds == 0 else self.prior[0, own]
            for i in range(n):
                t = t0 + i
                part = y[q * 48:(q + 1) * 48, i * L:(i + 1) * L]
                conv = pltpu.roll(part[:C] * column, 1, 1) + part[C:2 * C] + pltpu.roll(part[2 * C:] * column, L - 1, 1)
                self.totals[own] = self.totals[own] + self.steps[t:t + 1] * (self.state(t, own) + conv)
                emit(t, own, self.lat[own] + self.totals[own], self.totals[own])


def first_part(rounds, *refs):
    if rounds == 0:
        lat, from_a, own, mixed, swapped, w_conv, w_mid, w_out, kept_h, kept_s, done, w_in, steps, *rest = refs
        core = lax.axis_index("pix") % 2
        smalls = [(0, own[...]), (2, from_a[3]), (1 + 2 * core, mixed[...]), (3 - 2 * core, swapped[...])]
        tables(lax.axis_index("tm"), smalls, w_conv, w_in, steps, rest.pop())
        prior = None
    else:
        lat, from_a, prior, w_in, steps, w_mid, w_out, kept_h, kept_s, done, *rest = refs
    low, hid, sec = rest[:4], rest[4:8], rest[8:12]
    r = Round(rounds, lat, prior, from_a, w_in, w_mid, w_out, steps, low, 3)

    def emit(t, row, value, total):
        done[t + 1] = value
        if t == rounds:
            done[0] = total

    units = len(r.groups)
    for g in range(units + 2):
        if g < units:
            r.fill(g, list(range(3, 10)))
            r.hidden(g, 5, [(kept_h.at[g], 1), (hid[g], 0)])
            r.hidden(g, 7, [(hid[g], 1), (hid[g], 2)])
            r.hidden(g, 4, [(kept_h.at[g], 0)])
        if 0 < g <= units:
            k = g - 1
            r.second(k, 6, [(kept_h.at[k], 1, 1), (hid[k], 0, 3)], [(kept_s.at[k], 1), (sec[k], 0)])
            r.second(k, 5, [(kept_h.at[k], 0, 2), (hid[k], 0, 1)], [(kept_s.at[k], 0)])
        if g > 1:
            k = g - 2
            r.output(k, 3, 1, [(kept_s.at[k], 0, 2), (sec[k], 0, 1)], emit)


def second_part(rounds, *refs):
    lat, from_b = refs[:2]
    prior = refs[2] if rounds else None
    kept_h, kept_s, done, w_in, w_mid, w_out, steps, *rest = refs[3 if rounds else 2:]
    last = rounds == 2
    if last:
        out, rest = rest[:4], rest[4:]
        ready = rest.pop()
    else:
        nxt, to_a, to_b, *rest = rest
    low, hid, sec = rest[:4], rest[4:8], rest[8:12]
    r = Round(rounds, lat, prior, from_b, w_in, w_mid, w_out, steps, low, 0)
    core, tm = r.core, r.tm

    def keep(t, row, value):
        ready[pl.ds(((t // 2) ^ tm) * 128 + (t % 2) * 64 + row + core * (3 - 2 * row), C, stride=ROWS), :] = value

    def emit(t, row, value, total):
        if last:
            keep(t, row, value)
            return
        nxt[t + 1, row] = value
        if t == rounds:
            nxt[0, row] = total
        if t < TIMES - 1 and row < 3:
            to_b[t - rounds, row] = value.astype(BF)
        if t < TIMES - 1 and row > 0:
            to_a[t - rounds, 3 - row] = value.astype(BF)

    units = len(r.groups)
    for g in range(units + 2):
        if g < units:
            r.fill(g, list(range(6)))
            r.hidden(g, 2, [(hid[g], 1), (hid[g], 2)])
            r.hidden(g, 1, [(hid[g], 0)])
        if 0 < g <= units:
            k = g - 1
            r.second(k, 2, [(hid[k], 0, 3), (kept_h.at[k], 0, 1)], [(sec[k], 0), (sec[k], 1)])
            r.second(k, 4, [(hid[k], 2, 1), (kept_h.at[k], 0, 2)], [(sec[k], 2)])
        if g > 1:
            k = g - 2
            r.output(k, 0, 2, [(sec[k], 0, 3), (kept_s.at[k], 0, 1)], emit)
            r.output(k, 2, 1, [(sec[k], 2, 1), (kept_s.at[k], 0, 2)], emit)

    for t in range(rounds, TIMES):
        emit(t, 3, done[t + 1], done[0])
    for row in range(ROWS):
        if rounds == 1:
            nxt[1, row] = prior[1, row]
        if last:
            for t in range(2):
                keep(t, row, prior[t + 1, row])
    if last:
        for k in range(4):
            out[k][...] = ready[k * 128:(k + 1) * 128].reshape(32, ROWS, L)


def call(body, rounds, args, out_shape, scratch):
    return pl.pallas_call(
        functools.partial(body, rounds),
        out_shape=out_shape,
        in_specs=[VM] * len(args),
        out_specs=(VM,) * len(out_shape),
        scratch_shapes=scratch,
        compiler_params=pltpu.CompilerParams(vmem_limit_bytes=24 << 20),
    )(*args)


PAIR = (2 * F, 2 * L)


def scratch_of(low_rows, sec_rows):
    shapes = ((low_rows * 48, 2 * L), (3 * F, 2 * L), (sec_rows * F, 2 * L))
    return [pltpu.VMEM(shape, BF) for shape in shapes for _ in range(4)]


def run_first(rounds, *args):
    units = len(groups_of(rounds))
    out_shape = (jax.ShapeDtypeStruct((units,) + PAIR, BF),) * 2 + (jax.ShapeDtypeStruct((TIMES + 1, C, L), F32),)
    scratch = scratch_of(7, 1)
    if rounds == 0:
        out_shape += (jax.ShapeDtypeStruct((3 * F, 2 * F), BF), jax.ShapeDtypeStruct((TIMES, F), F32))
        scratch += [pltpu.VMEM((4, 16, F), F32)]
    return call(first_part, rounds, args, out_shape, scratch)


def run_second(rounds, *args):
    scratch = scratch_of(6, 3)
    if rounds == 2:
        out_shape = (jax.ShapeDtypeStruct((32, ROWS, L), F32),) * 4
        scratch += [pltpu.VMEM((512, L), F32)]
    else:
        sent = jax.ShapeDtypeStruct((TIMES - 1 - rounds, 3, C, L), BF)
        out_shape = (jax.ShapeDtypeStruct((TIMES + 1, ROWS, C, L), F32), sent, sent)
    return call(second_part, rounds, args, out_shape, scratch)


def join_body(p0, p1, p2, p3, out):
    tm = lax.axis_index("tm")
    pieces = [p0[...], p1[...], p2[...], p3[...]]
    lane = lax.broadcasted_iota(jnp.int32, pieces[0].shape, 2)
    placed = []
    for t in range(4):
        x = by_tm(t ^ tm, pieces)
        placed.append(pltpu.roll(x, STARTS[t] % L, 2))
    for g in range(3):
        out[:, :, g * L:(g + 1) * L] = jnp.where(lane < CUTS[g] - g * L, placed[g], placed[g + 1])
    out[:, :, 3 * L:] = placed[3][:, :, :448 - 3 * L]


def join(pieces):
    return pl.pallas_call(
        join_body,
        out_shape=jax.ShapeDtypeStruct((32, ROWS, 448), F32),
        in_specs=[VM] * 4,
        out_specs=VM,
        compiler_params=pltpu.CompilerParams(vmem_limit_bytes=8 << 20),
        name="join",
    )(*pieces)


def across(x, k):
    return lax.ppermute(x, "tm", [(t, t ^ k) for t in range(4)])


def pair_up(x, pairs):
    return lax.ppermute(x, "pix", [(a, b) for a, b in pairs] + [(b, a) for a, b in pairs])


def over_both(x, target):
    pixels = lax.axis_size("pix")
    pairs = []
    for t in range(4):
        for p in range(pixels):
            to_t, to_p = target(t, p)
            pairs.append((t * pixels + p, to_t * pixels + to_p))
    return lax.ppermute(x, ("tm", "pix"), pairs)


CORES = [(2 * k, 2 * k + 1) for k in range(32)]
CHIPS = [(2 * k + 1, 2 * k + 2) for k in range(31)]


def shards(latent, step_size, time_embed, conv_in, conv_mid, conv_out):
    lat, to_a, to_b, small = enter(step_size, latent, time_embed)
    mixed = over_both(small, lambda t, p: (t ^ (1 + 2 * (p % 2)), p))
    swapped = pair_up(mixed, CORES)
    smalls = [small, mixed, swapped]
    w_conv, w_mid, w_out = prepare(conv_in.transpose(0, 1, 3, 2), conv_mid, conv_out)
    prior = ()
    for rounds in range(3):
        from_b = pair_up(to_b, CHIPS)
        from_a = pair_up(to_a, CORES) if rounds else over_both(to_a, lambda t, p: (t ^ 2, p ^ 1))
        if rounds == 0:
            *kept, w_in, steps = run_first(0, lat, from_a, *smalls, w_conv, w_mid, w_out)
        else:
            kept = run_first(rounds, lat, from_a, *prior, w_in, steps, w_mid, w_out)
        done = run_second(rounds, lat, from_b, *prior, *kept, w_in, w_mid, w_out, steps)
        if rounds < 2:
            *prior, to_a, to_b = done
    got = [done[0]]
    for k in (1, 2, 3):
        got.append(across(done[k], k))
    return join(got).reshape(2, C, ROWS, 448)


def solution(mesh):
    in_specs = (P(None, "pix", None), P("tm"), P("tm", None), P(), P(), P())
    out_specs = P("tm", None, "pix", None)
    return jax.shard_map(shards, mesh=mesh, in_specs=in_specs, out_specs=out_specs, check_vma=False)
```

```python
import functools

import jax
import jax.numpy as jnp
from jax import lax
from jax.experimental import pallas as pl
from jax.experimental.pallas import tpu as pltpu
from jax.sharding import PartitionSpec as P


TIMES = 8
C = 16
F = 128
L = 128
ROWS = 4
STARTS = (-1, 105, 215, 321)
SHIFTS = tuple(-start % L for start in STARTS)
CUTS = (114, 224, 334)
BF = jnp.bfloat16
F32 = jnp.float32


VM = pl.BlockSpec(memory_space=pltpu.VMEM)
ANY = pl.BlockSpec(memory_space=pltpu.HBM)


def by_tm(tm, values):
    return jnp.where(tm == 0, values[0], jnp.where(tm == 1, values[1], jnp.where(tm == 2, values[2], values[3])))


def pieces_of(x):
    high = x.astype(BF).astype(F32)
    rest = x - high
    middle = rest.astype(BF).astype(F32)
    return high, middle, rest - middle


def enter_body(step, latent, embed, *refs):
    weights, (lat, to_a, to_b, small), fetched = refs[:3], refs[3:7], refs[7:10]
    step_s, latent_v, embed_v, other, sems = refs[10:]
    pairs = ((latent, latent_v), (embed, embed_v), (step, step_s), *zip(weights, fetched))
    copies = [pltpu.make_async_copy(x, y, sems.at[i]) for i, (x, y) in enumerate(pairs)]
    for copy in copies:
        copy.start()
    for copy in copies[:3]:
        copy.wait()
    tm, core = lax.axis_index("tm"), lax.axis_index("pix") % 2
    lane = lax.broadcasted_iota(jnp.int32, (C, L), 1)
    for r in range(ROWS):
        tiles = [jnp.zeros((C, L), F32)] + [latent_v[:, r, g * L:(g + 1) * L] for g in range(3)]
        tiles.append(jnp.concatenate([latent_v[:, r, 3 * L:], jnp.zeros((C, 4 * L - 448), F32)], axis=1))
        for t, to in ((tm, lat), (tm ^ 2, other)):
            shift = by_tm(t, SHIFTS)
            left, right = by_tm(t, tiles[:4]), by_tm(t, tiles[1:])
            to[r + core * (3 - 2 * r)] = jnp.where(lane < shift, pltpu.roll(left, shift, 1), pltpu.roll(right, shift, 1))
    for d in range(3):
        to_b[d] = lat[d].astype(BF)
        to_a[d] = other[3 - d].astype(BF)
    rows = jnp.concatenate([embed_v[...]] + [jnp.full((1, F), step_s[d], F32) for d in range(2)], axis=0)
    table = jnp.concatenate([*pieces_of(rows), jnp.zeros((4, F), F32)], axis=0).astype(BF)
    small[...] = table
    to_a[3] = table
    for copy in copies[3:]:
        copy.wait()


def enter(step, latent, embed, *weights):
    shapes = ((4, C, L), (3, C, L), (16, F)) + tuple(w.shape for w in weights)
    return pl.pallas_call(
        enter_body,
        out_shape=(jax.ShapeDtypeStruct((ROWS, C, L), F32),) + tuple(jax.ShapeDtypeStruct(shape, BF) for shape in shapes),
        in_specs=[ANY] * 6,
        out_specs=(VM,) * 7,
        scratch_shapes=[
            pltpu.SMEM((2,), F32),
            pltpu.VMEM((C, ROWS, 448), F32),
            pltpu.VMEM((2, F), F32),
            pltpu.VMEM((ROWS, C, L), F32),
            pltpu.SemaphoreType.DMA((6,)),
        ],
        compiler_params=pltpu.CompilerParams(vmem_limit_bytes=4 << 20),
        name="enter",
    )(*[pltpu.with_memory_space_constraint(v, pltpu.HBM) for v in (step, latent, embed, *weights)])


def prepare_body(in_v, mid_v, out_v, w_in, w_mid, w_out, turned):
    core = lax.axis_index("pix") % 2
    w_mid[...] = jnp.zeros_like(w_mid)
    w_out[...] = jnp.zeros_like(w_out)
    turned[...] = jnp.zeros_like(turned)
    for a in range(3):
        row = a + core * (2 - 2 * a)
        for b in range(3):
            mid = mid_v[row, b] * 0.5
            tail = out_v[row, b]
            head = in_v[row, b] * 0.5
            for q in range(2):
                w_mid[(b * 2 + q) * F:(b * 2 + q + 1) * F, (a + q) * F:(a + q + 1) * F] = mid
                w_out[q * 48 + b * C:q * 48 + (b + 1) * C, (a + q) * F:(a + q + 1) * F] = tail
                turned[(a + q) * 48 + b * C:(a + q) * 48 + (b + 1) * C, q * F:(q + 1) * F] = head
    w_in[:2 * F] = turned[...].astype(F32).T.astype(BF)
    w_in[2 * F:] = jnp.zeros((F, 2 * F), BF)


def prepare(conv_in, conv_mid, conv_out):
    shapes = ((3 * F, 2 * F), (7 * F, 4 * F), (96, 4 * F))
    return pl.pallas_call(
        prepare_body,
        out_shape=tuple(jax.ShapeDtypeStruct(shape, BF) for shape in shapes),
        in_specs=[VM] * 3,
        out_specs=(VM,) * 3,
        scratch_shapes=[
            pltpu.VMEM((2 * F, 2 * F), BF),
        ],
        compiler_params=pltpu.CompilerParams(vmem_limit_bytes=8 << 20),
        name="prepare",
    )(conv_in, conv_mid, conv_out)


def tables(tm, smalls, w_conv, w_in, steps, gathered):
    for k, small in smalls:
        gathered[tm ^ k] = small.astype(F32)
    high, middle, rest = [jnp.concatenate([gathered[t, at:at + 2] for t in range(4)], axis=0) * 0.5 for at in (0, 4, 8)]
    steps[...] = sum(jnp.concatenate([gathered[t, at:at + 2] for t in range(4)], axis=0) for at in (2, 6, 10))
    tail = jnp.concatenate([jnp.zeros((64, F), F32), high, middle, rest, jnp.zeros((40, F), F32)], axis=0)
    tail = tail.T.astype(BF)
    w_in[:, :F] = w_conv[:, :F]
    for q in range(2):
        w_in[q * F:(q + 1) * F, F:] = w_conv[q * F:(q + 1) * F, F:] + tail
    w_in[2 * F:, F:] = w_conv[2 * F:, F:]


def silu2(v):
    return v + v * jnp.tanh(v)


def groups_of(rounds):
    return [(t0, min(2, TIMES - t0)) for t0 in range(rounds, TIMES, 2)]


class Round:
    def __init__(self, rounds, lat, prior, halo, w_in, w_mid, w_out, steps, low, first_row):
        self.rounds, self.lat, self.prior, self.halo = rounds, lat, prior, halo
        self.w_in, self.w_mid, self.w_out, self.steps = w_in, w_mid, w_out, steps
        self.low, self.first_row = low, first_row
        pix, self.tm = lax.axis_index("pix"), lax.axis_index("tm")
        self.core = pix % 2
        self.inside = (pix > 0) & (pix < 63)
        self.groups = groups_of(rounds)
        lane = lax.broadcasted_iota(jnp.int32, (C, L), 1)
        self.column = jnp.where(((self.tm == 0) & (lane == 0)) | ((self.tm == 3) & (lane == L - 1)), 0.0, 1.0)
        self.totals = {}

    def state(self, t, row):
        return self.lat[row] if self.rounds == 0 else self.prior[t, row]

    def fill(self, g, rows):
        t0, n = self.groups[g]
        rounds, column = self.rounds, self.column
        for w in rows:
            for i in range(n if rounds else 1):
                if 3 <= w < 7:
                    x = self.state(t0 + i, w - 3)
                else:
                    d = 2 - w if w < 3 else w - 7
                    x = self.halo[(t0 + i - rounds, d) if rounds else (d,)].astype(F32)
                x = x * column
                x = jnp.concatenate([pltpu.roll(x, 1, 1) * column, x, pltpu.roll(x, L - 1, 1) * column], axis=0).astype(BF)
                at = (w - self.first_row) * 48
                for lanes in ([i] if rounds else range(n)):
                    self.low[g][at:at + 48, lanes * L:(lanes + 1) * L] = x

    def block(self, row, last, normal, zero):
        return normal * F if row > last else pl.multiple_of(jnp.where(self.inside, normal * F, zero * F), F)

    def hidden(self, g, row, to):
        t0, n = self.groups[g]
        width = n * L
        r = lax.broadcasted_iota(jnp.int32, (64, width), 0)
        c = lax.broadcasted_iota(jnp.int32, (64, width), 1)
        edge = ((self.tm == 0) & ((c & 127) == 0)) | ((self.tm == 3) & ((c & 127) == L - 1))
        pick = jnp.where(((r & 7) == t0 + (c >> 7)) & (r < 24) & jnp.logical_not(edge), 1.0, 0.0).astype(BF)
        at = (row - 1 - self.first_row) * 48
        rhs = jnp.concatenate([self.low[g][at:at + 192, :width], pick], axis=0)
        blocks = [self.w_in[pl.ds(self.block(row + q, 2, q, 2), F), :] for q in range(len(to))]
        v = silu2(jnp.dot(jnp.concatenate(blocks, axis=0), rhs, preferred_element_type=F32)).astype(BF)
        for q, (ref, place) in enumerate(to):
            ref[place * F:(place + 1) * F, :width] = v[q * F:(q + 1) * F]

    def second(self, g, row, sources, to):
        _, n = self.groups[g]
        count = len(to)
        rhs = jnp.concatenate([ref[at * F:(at + k) * F, :n * L] for ref, at, k in sources], axis=0)
        depth = (count + 2) * F
        blocks = [self.w_mid[pl.ds(self.block(row + q, 2, 2 * b + q, 6), F), :depth] for b in range(3) for q in range(count)]
        y = jnp.dot(jnp.concatenate(blocks, axis=0), rhs, preferred_element_type=F32)
        m = count * F
        for i in range(n):
            lanes = slice(i * L, (i + 1) * L)
            part = y[:, lanes]
            v = pltpu.roll(part[:m], 1, 1) + part[m:2 * m] + pltpu.roll(part[2 * m:], L - 1, 1)
            v = silu2(v).astype(BF)
            for q, (ref, place) in enumerate(to):
                ref[place * F:(place + 1) * F, lanes] = v[q * F:(q + 1) * F]

    def output(self, g, row, count, sources, emit):
        t0, n = self.groups[g]
        column = self.column
        rhs = jnp.concatenate([ref[at * F:(at + k) * F, :n * L] for ref, at, k in sources], axis=0)
        y = jnp.dot(self.w_out[:count * 48, :(count + 2) * F], rhs, preferred_element_type=F32)
        for q in range(count):
            own = row + q
            if own not in self.totals:
                self.totals[own] = jnp.zeros((C, L), F32) if self.rounds == 0 else self.prior[0, own]
            for i in range(n):
                t = t0 + i
                part = y[q * 48:(q + 1) * 48, i * L:(i + 1) * L]
                conv = pltpu.roll(part[:C] * column, 1, 1) + part[C:2 * C] + pltpu.roll(part[2 * C:] * column, L - 1, 1)
                self.totals[own] = self.totals[own] + self.steps[t:t + 1] * (self.state(t, own) + conv)
                emit(t, own, self.lat[own] + self.totals[own], self.totals[own])


def first_part(rounds, *refs):
    if rounds == 0:
        lat, from_a, own, mixed, swapped, w_conv, w_mid, w_out, kept_h, kept_s, done, w_in, steps, *rest = refs
        core = lax.axis_index("pix") % 2
        smalls = [(0, own[...]), (2, from_a[3]), (1 + 2 * core, mixed[...]), (3 - 2 * core, swapped[...])]
        tables(lax.axis_index("tm"), smalls, w_conv, w_in, steps, rest.pop())
        prior = None
    else:
        lat, from_a, prior, w_in, steps, w_mid, w_out, kept_h, kept_s, done, *rest = refs
    low, hid, sec = rest[:4], rest[4:8], rest[8:12]
    r = Round(rounds, lat, prior, from_a, w_in, w_mid, w_out, steps, low, 3)

    def emit(t, row, value, total):
        done[t + 1] = value
        if t == rounds:
            done[0] = total

    units = len(r.groups)
    for g in range(units + 2):
        if g < units:
            r.fill(g, list(range(3, 10)))
            r.hidden(g, 5, [(kept_h.at[g], 1), (hid[g], 0)])
            r.hidden(g, 7, [(hid[g], 1), (hid[g], 2)])
            r.hidden(g, 4, [(kept_h.at[g], 0)])
        if 0 < g <= units:
            k = g - 1
            r.second(k, 6, [(kept_h.at[k], 1, 1), (hid[k], 0, 3)], [(kept_s.at[k], 1), (sec[k], 0)])
            r.second(k, 5, [(kept_h.at[k], 0, 2), (hid[k], 0, 1)], [(kept_s.at[k], 0)])
        if g > 1:
            k = g - 2
            r.output(k, 3, 1, [(kept_s.at[k], 0, 2), (sec[k], 0, 1)], emit)


def second_part(rounds, *refs):
    lat, from_b = refs[:2]
    prior = refs[2] if rounds else None
    kept_h, kept_s, done, w_in, w_mid, w_out, steps, *rest = refs[3 if rounds else 2:]
    last = rounds == 2
    if last:
        out, rest = rest[:4], rest[4:]
        ready = rest.pop()
    else:
        nxt, to_a, to_b, *rest = rest
    low, hid, sec = rest[:4], rest[4:8], rest[8:12]
    r = Round(rounds, lat, prior, from_b, w_in, w_mid, w_out, steps, low, 0)
    core, tm = r.core, r.tm

    def keep(t, row, value):
        ready[pl.ds(((t // 2) ^ tm) * 128 + (t % 2) * 64 + row + core * (3 - 2 * row), C, stride=ROWS), :] = value

    def emit(t, row, value, total):
        if last:
            keep(t, row, value)
            return
        nxt[t + 1, row] = value
        if t == rounds:
            nxt[0, row] = total
        if t < TIMES - 1 and row < 3:
            to_b[t - rounds, row] = value.astype(BF)
        if t < TIMES - 1 and row > 0:
            to_a[t - rounds, 3 - row] = value.astype(BF)

    units = len(r.groups)
    for g in range(units + 2):
        if g < units:
            r.fill(g, list(range(6)))
            r.hidden(g, 2, [(hid[g], 1), (hid[g], 2)])
            r.hidden(g, 1, [(hid[g], 0)])
        if 0 < g <= units:
            k = g - 1
            r.second(k, 2, [(hid[k], 0, 3), (kept_h.at[k], 0, 1)], [(sec[k], 0), (sec[k], 1)])
            r.second(k, 4, [(hid[k], 2, 1), (kept_h.at[k], 0, 2)], [(sec[k], 2)])
        if g > 1:
            k = g - 2
            r.output(k, 0, 2, [(sec[k], 0, 3), (kept_s.at[k], 0, 1)], emit)
            r.output(k, 2, 1, [(sec[k], 2, 1), (kept_s.at[k], 0, 2)], emit)

    for t in range(rounds, TIMES):
        emit(t, 3, done[t + 1], done[0])
    for row in range(ROWS):
        if rounds == 1:
            nxt[1, row] = prior[1, row]
        if last:
            for t in range(2):
                keep(t, row, prior[t + 1, row])
    if last:
        for k in range(4):
            out[k][...] = ready[k * 128:(k + 1) * 128].reshape(32, ROWS, L)


def call(body, rounds, args, out_shape, scratch):
    return pl.pallas_call(
        functools.partial(body, rounds),
        out_shape=out_shape,
        in_specs=[VM] * len(args),
        out_specs=(VM,) * len(out_shape),
        scratch_shapes=scratch,
        compiler_params=pltpu.CompilerParams(vmem_limit_bytes=24 << 20),
    )(*args)


PAIR = (2 * F, 2 * L)


def scratch_of(low_rows, sec_rows):
    shapes = ((low_rows * 48, 2 * L), (3 * F, 2 * L), (sec_rows * F, 2 * L))
    return [pltpu.VMEM(shape, BF) for shape in shapes for _ in range(4)]


def run_first(rounds, *args):
    units = len(groups_of(rounds))
    out_shape = (jax.ShapeDtypeStruct((units,) + PAIR, BF),) * 2 + (jax.ShapeDtypeStruct((TIMES + 1, C, L), F32),)
    scratch = scratch_of(7, 1)
    if rounds == 0:
        out_shape += (jax.ShapeDtypeStruct((3 * F, 2 * F), BF), jax.ShapeDtypeStruct((TIMES, F), F32))
        scratch += [pltpu.VMEM((4, 16, F), F32)]
    return call(first_part, rounds, args, out_shape, scratch)


def run_second(rounds, *args):
    scratch = scratch_of(6, 3)
    if rounds == 2:
        out_shape = (jax.ShapeDtypeStruct((32, ROWS, L), F32),) * 4
        scratch += [pltpu.VMEM((512, L), F32)]
    else:
        sent = jax.ShapeDtypeStruct((TIMES - 1 - rounds, 3, C, L), BF)
        out_shape = (jax.ShapeDtypeStruct((TIMES + 1, ROWS, C, L), F32), sent, sent)
    return call(second_part, rounds, args, out_shape, scratch)


def join_body(p0, p1, p2, p3, out):
    tm = lax.axis_index("tm")
    pieces = [p0[...], p1[...], p2[...], p3[...]]
    lane = lax.broadcasted_iota(jnp.int32, pieces[0].shape, 2)
    placed = []
    for t in range(4):
        x = by_tm(t ^ tm, pieces)
        placed.append(pltpu.roll(x, STARTS[t] % L, 2))
    for g in range(3):
        out[:, :, g * L:(g + 1) * L] = jnp.where(lane < CUTS[g] - g * L, placed[g], placed[g + 1])
    out[:, :, 3 * L:] = placed[3][:, :, :448 - 3 * L]


def join(pieces):
    return pl.pallas_call(
        join_body,
        out_shape=jax.ShapeDtypeStruct((32, ROWS, 448), F32),
        in_specs=[VM] * 4,
        out_specs=VM,
        compiler_params=pltpu.CompilerParams(vmem_limit_bytes=8 << 20),
        name="join",
    )(*pieces)


def across(x, k):
    return lax.ppermute(x, "tm", [(t, t ^ k) for t in range(4)])


def pair_up(x, pairs):
    return lax.ppermute(x, "pix", [(a, b) for a, b in pairs] + [(b, a) for a, b in pairs])


def over_both(x, target):
    pixels = lax.axis_size("pix")
    pairs = []
    for t in range(4):
        for p in range(pixels):
            to_t, to_p = target(t, p)
            pairs.append((t * pixels + p, to_t * pixels + to_p))
    return lax.ppermute(x, ("tm", "pix"), pairs)


CORES = [(2 * k, 2 * k + 1) for k in range(32)]
CHIPS = [(2 * k + 1, 2 * k + 2) for k in range(31)]


def shards(latent, step_size, time_embed, conv_in, conv_mid, conv_out):
    lat, to_a, to_b, small, *weights = enter(step_size, latent, time_embed, conv_in.transpose(0, 1, 3, 2), conv_mid, conv_out)
    mixed = over_both(small, lambda t, p: (t ^ (1 + 2 * (p % 2)), p))
    swapped = pair_up(mixed, CORES)
    smalls = [small, mixed, swapped]
    w_conv, w_mid, w_out = prepare(*weights)
    prior = ()
    for rounds in range(3):
        from_b = pair_up(to_b, CHIPS)
        from_a = pair_up(to_a, CORES) if rounds else over_both(to_a, lambda t, p: (t ^ 2, p ^ 1))
        if rounds == 0:
            *kept, w_in, steps = run_first(0, lat, from_a, *smalls, w_conv, w_mid, w_out)
        else:
            kept = run_first(rounds, lat, from_a, *prior, w_in, steps, w_mid, w_out)
        done = run_second(rounds, lat, from_b, *prior, *kept, w_in, w_mid, w_out, steps)
        if rounds < 2:
            *prior, to_a, to_b = done
    got = [done[0]]
    for k in (1, 2, 3):
        got.append(across(done[k], k))
    return join(got).reshape(2, C, ROWS, 448)


def solution(mesh):
    in_specs = (P(None, "pix", None), P("tm"), P("tm", None), P(), P(), P())
    out_specs = P("tm", None, "pix", None)
    return jax.shard_map(shards, mesh=mesh, in_specs=in_specs, out_specs=out_specs, check_vma=False)
```

```python
import functools

import jax
import jax.numpy as jnp
from jax import lax
from jax.experimental import pallas as pl
from jax.experimental.pallas import tpu as pltpu
from jax.sharding import PartitionSpec as P


TIMES = 8
C = 16
F = 128
L = 128
ROWS = 4
STARTS = (-1, 105, 215, 321)
SHIFTS = tuple(-start % L for start in STARTS)
CUTS = (114, 224, 334)
BF = jnp.bfloat16
F32 = jnp.float32


VM = pl.BlockSpec(memory_space=pltpu.VMEM)
ANY = pl.BlockSpec(memory_space=pltpu.HBM)


def by_tm(tm, values):
    return jnp.where(tm == 0, values[0], jnp.where(tm == 1, values[1], jnp.where(tm == 2, values[2], values[3])))


def pieces_of(x):
    high = x.astype(BF).astype(F32)
    rest = x - high
    middle = rest.astype(BF).astype(F32)
    return high, middle, rest - middle


def enter_body(step, latent, embed, lat, to_a, to_b, small, step_s, latent_v, embed_v, other, sems):
    copies = [pltpu.make_async_copy(x, y, sems.at[i]) for i, (x, y) in enumerate(((latent, latent_v), (embed, embed_v), (step, step_s)))]
    for copy in copies:
        copy.start()
    for copy in copies:
        copy.wait()
    tm, core = lax.axis_index("tm"), lax.axis_index("pix") % 2
    lane = lax.broadcasted_iota(jnp.int32, (C, L), 1)
    for r in range(ROWS):
        tiles = [jnp.zeros((C, L), F32)] + [latent_v[:, r, g * L:(g + 1) * L] for g in range(3)]
        tiles.append(jnp.concatenate([latent_v[:, r, 3 * L:], jnp.zeros((C, 4 * L - 448), F32)], axis=1))
        for t, to in ((tm, lat), (tm ^ 2, other)):
            shift = by_tm(t, SHIFTS)
            left, right = by_tm(t, tiles[:4]), by_tm(t, tiles[1:])
            to[r + core * (3 - 2 * r)] = jnp.where(lane < shift, pltpu.roll(left, shift, 1), pltpu.roll(right, shift, 1))
    for d in range(3):
        to_b[d] = lat[d].astype(BF)
        to_a[d] = other[3 - d].astype(BF)
    rows = jnp.concatenate([embed_v[...]] + [jnp.full((1, F), step_s[d], F32) for d in range(2)], axis=0)
    table = jnp.concatenate([*pieces_of(rows), jnp.zeros((4, F), F32)], axis=0).astype(BF)
    small[...] = table
    to_a[3] = table


def enter(step, latent, embed):
    shapes = ((4, C, L), (3, C, L), (16, F))
    return pl.pallas_call(
        enter_body,
        out_shape=(jax.ShapeDtypeStruct((ROWS, C, L), F32),) + tuple(jax.ShapeDtypeStruct(shape, BF) for shape in shapes),
        in_specs=[ANY] * 3,
        out_specs=(VM,) * 4,
        scratch_shapes=[
            pltpu.SMEM((2,), F32),
            pltpu.VMEM((C, ROWS, 448), F32),
            pltpu.VMEM((2, F), F32),
            pltpu.VMEM((ROWS, C, L), F32),
            pltpu.SemaphoreType.DMA((3,)),
        ],
        compiler_params=pltpu.CompilerParams(vmem_limit_bytes=4 << 20),
        name="enter",
    )(*[pltpu.with_memory_space_constraint(v, pltpu.HBM) for v in (step, latent, embed)])


def prepare_body(conv_in, conv_mid, conv_out, w_in, w_mid, w_out, in_v, mid_v, out_v, turned, sems):
    copies = [pltpu.make_async_copy(x, y, sems.at[i]) for i, (x, y) in enumerate(((conv_in, in_v), (conv_mid, mid_v), (conv_out, out_v)))]
    for copy in copies:
        copy.start()
    core = lax.axis_index("pix") % 2
    w_mid[...] = jnp.zeros_like(w_mid)
    w_out[...] = jnp.zeros_like(w_out)
    turned[...] = jnp.zeros_like(turned)
    for copy in copies:
        copy.wait()
    for a in range(3):
        row = a + core * (2 - 2 * a)
        for b in range(3):
            mid = mid_v[row, b] * 0.5
            tail = out_v[row, b]
            head = in_v[row, b] * 0.5
            for q in range(2):
                w_mid[(b * 2 + q) * F:(b * 2 + q + 1) * F, (a + q) * F:(a + q + 1) * F] = mid
                w_out[q * 48 + b * C:q * 48 + (b + 1) * C, (a + q) * F:(a + q + 1) * F] = tail
                turned[(a + q) * 48 + b * C:(a + q) * 48 + (b + 1) * C, q * F:(q + 1) * F] = head
    w_in[:2 * F] = turned[...].astype(F32).T.astype(BF)
    w_in[2 * F:] = jnp.zeros((F, 2 * F), BF)


def prepare(conv_in, conv_mid, conv_out):
    shapes = ((3 * F, 2 * F), (7 * F, 4 * F), (96, 4 * F))
    return pl.pallas_call(
        prepare_body,
        out_shape=tuple(jax.ShapeDtypeStruct(shape, BF) for shape in shapes),
        in_specs=[ANY] * 3,
        out_specs=(VM,) * 3,
        scratch_shapes=[
            pltpu.VMEM((3, 3, C, F), BF),
            pltpu.VMEM((3, 3, F, F), BF),
            pltpu.VMEM((3, 3, C, F), BF),
            pltpu.VMEM((2 * F, 2 * F), BF),
            pltpu.SemaphoreType.DMA((3,)),
        ],
        compiler_params=pltpu.CompilerParams(vmem_limit_bytes=8 << 20),
        name="prepare",
    )(*[pltpu.with_memory_space_constraint(v, pltpu.HBM) for v in (conv_in, conv_mid, conv_out)])


def tables(tm, smalls, w_conv, w_in, steps, gathered):
    for k, small in smalls:
        gathered[tm ^ k] = small.astype(F32)
    high, middle, rest = [jnp.concatenate([gathered[t, at:at + 2] for t in range(4)], axis=0) * 0.5 for at in (0, 4, 8)]
    steps[...] = sum(jnp.concatenate([gathered[t, at:at + 2] for t in range(4)], axis=0) for at in (2, 6, 10))
    tail = jnp.concatenate([jnp.zeros((64, F), F32), high, middle, rest, jnp.zeros((40, F), F32)], axis=0)
    tail = tail.T.astype(BF)
    w_in[:, :F] = w_conv[:, :F]
    for q in range(2):
        w_in[q * F:(q + 1) * F, F:] = w_conv[q * F:(q + 1) * F, F:] + tail
    w_in[2 * F:, F:] = w_conv[2 * F:, F:]


def silu2(v):
    return v + v * jnp.tanh(v)


def groups_of(rounds):
    return [(t0, min(2, TIMES - t0)) for t0 in range(rounds, TIMES, 2)]


class Round:
    def __init__(self, rounds, lat, prior, halo, w_in, w_mid, w_out, steps, low, first_row):
        self.rounds, self.lat, self.prior, self.halo = rounds, lat, prior, halo
        self.w_in, self.w_mid, self.w_out, self.steps = w_in, w_mid, w_out, steps
        self.low, self.first_row = low, first_row
        pix, self.tm = lax.axis_index("pix"), lax.axis_index("tm")
        self.core = pix % 2
        self.inside = (pix > 0) & (pix < 63)
        self.groups = groups_of(rounds)
        lane = lax.broadcasted_iota(jnp.int32, (C, L), 1)
        self.column = jnp.where(((self.tm == 0) & (lane == 0)) | ((self.tm == 3) & (lane == L - 1)), 0.0, 1.0)
        self.totals = {}

    def state(self, t, row):
        return self.lat[row] if self.rounds == 0 else self.prior[t, row]

    def fill(self, g, rows):
        t0, n = self.groups[g]
        rounds, column = self.rounds, self.column
        for w in rows:
            for i in range(n if rounds else 1):
                if 3 <= w < 7:
                    x = self.state(t0 + i, w - 3)
                else:
                    d = 2 - w if w < 3 else w - 7
                    x = self.halo[(t0 + i - rounds, d) if rounds else (d,)].astype(F32)
                x = x * column
                x = jnp.concatenate([pltpu.roll(x, 1, 1) * column, x, pltpu.roll(x, L - 1, 1) * column], axis=0).astype(BF)
                at = (w - self.first_row) * 48
                for lanes in ([i] if rounds else range(n)):
                    self.low[g][at:at + 48, lanes * L:(lanes + 1) * L] = x

    def block(self, row, last, normal, zero):
        return normal * F if row > last else pl.multiple_of(jnp.where(self.inside, normal * F, zero * F), F)

    def hidden(self, g, row, to):
        t0, n = self.groups[g]
        width = n * L
        r = lax.broadcasted_iota(jnp.int32, (64, width), 0)
        c = lax.broadcasted_iota(jnp.int32, (64, width), 1)
        edge = ((self.tm == 0) & ((c & 127) == 0)) | ((self.tm == 3) & ((c & 127) == L - 1))
        pick = jnp.where(((r & 7) == t0 + (c >> 7)) & (r < 24) & jnp.logical_not(edge), 1.0, 0.0).astype(BF)
        at = (row - 1 - self.first_row) * 48
        rhs = jnp.concatenate([self.low[g][at:at + 192, :width], pick], axis=0)
        blocks = [self.w_in[pl.ds(self.block(row + q, 2, q, 2), F), :] for q in range(len(to))]
        v = silu2(jnp.dot(jnp.concatenate(blocks, axis=0), rhs, preferred_element_type=F32)).astype(BF)
        for q, (ref, place) in enumerate(to):
            ref[place * F:(place + 1) * F, :width] = v[q * F:(q + 1) * F]

    def second(self, g, row, sources, to):
        _, n = self.groups[g]
        count = len(to)
        rhs = jnp.concatenate([ref[at * F:(at + k) * F, :n * L] for ref, at, k in sources], axis=0)
        depth = (count + 2) * F
        blocks = [self.w_mid[pl.ds(self.block(row + q, 2, 2 * b + q, 6), F), :depth] for b in range(3) for q in range(count)]
        y = jnp.dot(jnp.concatenate(blocks, axis=0), rhs, preferred_element_type=F32)
        m = count * F
        for i in range(n):
            lanes = slice(i * L, (i + 1) * L)
            part = y[:, lanes]
            v = pltpu.roll(part[:m], 1, 1) + part[m:2 * m] + pltpu.roll(part[2 * m:], L - 1, 1)
            v = silu2(v).astype(BF)
            for q, (ref, place) in enumerate(to):
                ref[place * F:(place + 1) * F, lanes] = v[q * F:(q + 1) * F]

    def output(self, g, row, count, sources, emit):
        t0, n = self.groups[g]
        column = self.column
        rhs = jnp.concatenate([ref[at * F:(at + k) * F, :n * L] for ref, at, k in sources], axis=0)
        y = jnp.dot(self.w_out[:count * 48, :(count + 2) * F], rhs, preferred_element_type=F32)
        for q in range(count):
            own = row + q
            if own not in self.totals:
                self.totals[own] = jnp.zeros((C, L), F32) if self.rounds == 0 else self.prior[0, own]
            for i in range(n):
                t = t0 + i
                part = y[q * 48:(q + 1) * 48, i * L:(i + 1) * L]
                conv = pltpu.roll(part[:C] * column, 1, 1) + part[C:2 * C] + pltpu.roll(part[2 * C:] * column, L - 1, 1)
                self.totals[own] = self.totals[own] + self.steps[t:t + 1] * (self.state(t, own) + conv)
                emit(t, own, self.lat[own] + self.totals[own], self.totals[own])


def first_part(rounds, *refs):
    if rounds == 0:
        lat, from_a, own, mixed, swapped, w_conv, w_mid, w_out, kept_h, kept_s, done, w_in, steps, *rest = refs
        core = lax.axis_index("pix") % 2
        smalls = [(0, own[...]), (2, from_a[3]), (1 + 2 * core, mixed[...]), (3 - 2 * core, swapped[...])]
        tables(lax.axis_index("tm"), smalls, w_conv, w_in, steps, rest.pop())
        prior = None
    else:
        lat, from_a, prior, w_in, steps, w_mid, w_out, kept_h, kept_s, done, *rest = refs
    low, hid, sec = rest[:4], rest[4:8], rest[8:12]
    r = Round(rounds, lat, prior, from_a, w_in, w_mid, w_out, steps, low, 3)

    def emit(t, row, value, total):
        done[t + 1] = value
        if t == rounds:
            done[0] = total

    units = len(r.groups)
    for g in range(units + 2):
        if g < units:
            r.fill(g, list(range(3, 10)))
            r.hidden(g, 5, [(kept_h.at[g], 1), (hid[g], 0)])
            r.hidden(g, 7, [(hid[g], 1), (hid[g], 2)])
            r.hidden(g, 4, [(kept_h.at[g], 0)])
        if 0 < g <= units:
            k = g - 1
            r.second(k, 6, [(kept_h.at[k], 1, 1), (hid[k], 0, 3)], [(kept_s.at[k], 1), (sec[k], 0)])
            r.second(k, 5, [(kept_h.at[k], 0, 2), (hid[k], 0, 1)], [(kept_s.at[k], 0)])
        if g > 1:
            k = g - 2
            r.output(k, 3, 1, [(kept_s.at[k], 0, 2), (sec[k], 0, 1)], emit)


def second_part(rounds, *refs):
    lat, from_b = refs[:2]
    prior = refs[2] if rounds else None
    kept_h, kept_s, done, w_in, w_mid, w_out, steps, *rest = refs[3 if rounds else 2:]
    last = rounds == 2
    if last:
        out, rest = rest[:4], rest[4:]
        ready = rest.pop()
    else:
        nxt, to_a, to_b, *rest = rest
    low, hid, sec = rest[:4], rest[4:8], rest[8:12]
    r = Round(rounds, lat, prior, from_b, w_in, w_mid, w_out, steps, low, 0)
    core, tm = r.core, r.tm

    def keep(t, row, value):
        ready[pl.ds(((t // 2) ^ tm) * 128 + (t % 2) * 64 + row + core * (3 - 2 * row), C, stride=ROWS), :] = value

    def emit(t, row, value, total):
        if last:
            keep(t, row, value)
            return
        nxt[t + 1, row] = value
        if t == rounds:
            nxt[0, row] = total
        if t < TIMES - 1 and row < 3:
            to_b[t - rounds, row] = value.astype(BF)
        if t < TIMES - 1 and row > 0:
            to_a[t - rounds, 3 - row] = value.astype(BF)

    units = len(r.groups)
    for g in range(units + 2):
        if g < units:
            r.fill(g, list(range(5)))
            r.hidden(g, 2, [(hid[g], 1), (hid[g], 2)])
            r.hidden(g, 1, [(hid[g], 0)])
        if 0 < g <= units:
            k = g - 1
            r.second(k, 4, [(hid[k], 2, 1), (kept_h.at[k], 0, 2)], [(sec[k], 2)])
            r.second(k, 2, [(hid[k], 0, 3), (kept_h.at[k], 0, 1)], [(sec[k], 0), (sec[k], 1)])
        if g > 1:
            k = g - 2
            r.output(k, 2, 1, [(sec[k], 2, 1), (kept_s.at[k], 0, 2)], emit)
            r.output(k, 0, 2, [(sec[k], 0, 3), (kept_s.at[k], 0, 1)], emit)

    for t in range(rounds, TIMES):
        emit(t, 3, done[t + 1], done[0])
    for row in range(ROWS):
        if rounds == 1:
            nxt[1, row] = prior[1, row]
        if last:
            for t in range(2):
                keep(t, row, prior[t + 1, row])
    if last:
        for k in range(4):
            out[k][...] = ready[k * 128:(k + 1) * 128].reshape(32, ROWS, L)


def call(body, rounds, args, out_shape, scratch):
    return pl.pallas_call(
        functools.partial(body, rounds),
        out_shape=out_shape,
        in_specs=[VM] * len(args),
        out_specs=(VM,) * len(out_shape),
        scratch_shapes=scratch,
        compiler_params=pltpu.CompilerParams(vmem_limit_bytes=24 << 20),
    )(*args)


PAIR = (2 * F, 2 * L)


def scratch_of(low_rows, sec_rows):
    shapes = ((low_rows * 48, 2 * L), (3 * F, 2 * L), (sec_rows * F, 2 * L))
    return [pltpu.VMEM(shape, BF) for shape in shapes for _ in range(4)]


def run_first(rounds, *args):
    units = len(groups_of(rounds))
    out_shape = (jax.ShapeDtypeStruct((units,) + PAIR, BF),) * 2 + (jax.ShapeDtypeStruct((TIMES + 1, C, L), F32),)
    scratch = scratch_of(7, 1)
    if rounds == 0:
        out_shape += (jax.ShapeDtypeStruct((3 * F, 2 * F), BF), jax.ShapeDtypeStruct((TIMES, F), F32))
        scratch += [pltpu.VMEM((4, 16, F), F32)]
    return call(first_part, rounds, args, out_shape, scratch)


def run_second(rounds, *args):
    scratch = scratch_of(5, 3)
    if rounds == 2:
        out_shape = (jax.ShapeDtypeStruct((32, ROWS, L), F32),) * 4
        scratch += [pltpu.VMEM((520, L), F32)]
    else:
        sent = jax.ShapeDtypeStruct((TIMES - 1 - rounds, 3, C, L), BF)
        out_shape = (jax.ShapeDtypeStruct((TIMES + 1, ROWS, C, L), F32), sent, sent)
    return call(second_part, rounds, args, out_shape, scratch)


def join_body(p0, p1, p2, p3, out):
    tm = lax.axis_index("tm")
    pieces = [p0[...], p1[...], p2[...], p3[...]]
    lane = lax.broadcasted_iota(jnp.int32, pieces[0].shape, 2)
    placed = []
    for t in range(4):
        x = by_tm(t ^ tm, pieces)
        placed.append(pltpu.roll(x, STARTS[t] % L, 2))
    for g in range(3):
        out[:, :, g * L:(g + 1) * L] = jnp.where(lane < CUTS[g] - g * L, placed[g], placed[g + 1])
    out[:, :, 3 * L:] = placed[3][:, :, :448 - 3 * L]


def join(pieces):
    return pl.pallas_call(
        join_body,
        out_shape=jax.ShapeDtypeStruct((32, ROWS, 448), F32),
        in_specs=[VM] * 4,
        out_specs=VM,
        compiler_params=pltpu.CompilerParams(vmem_limit_bytes=8 << 20),
        name="join",
    )(*pieces)


def across(x, k):
    return lax.ppermute(x, "tm", [(t, t ^ k) for t in range(4)])


def pair_up(x, pairs):
    return lax.ppermute(x, "pix", [(a, b) for a, b in pairs] + [(b, a) for a, b in pairs])


def over_both(x, target):
    pixels = lax.axis_size("pix")
    pairs = []
    for t in range(4):
        for p in range(pixels):
            to_t, to_p = target(t, p)
            pairs.append((t * pixels + p, to_t * pixels + to_p))
    return lax.ppermute(x, ("tm", "pix"), pairs)


CORES = [(2 * k, 2 * k + 1) for k in range(32)]
CHIPS = [(2 * k + 1, 2 * k + 2) for k in range(31)]


def shards(latent, step_size, time_embed, conv_in, conv_mid, conv_out):
    lat, to_a, to_b, small = enter(step_size, latent, time_embed)
    mixed = over_both(small, lambda t, p: (t ^ (1 + 2 * (p % 2)), p))
    swapped = pair_up(mixed, CORES)
    smalls = [small, mixed, swapped]
    w_conv, w_mid, w_out = prepare(conv_in.transpose(0, 1, 3, 2), conv_mid, conv_out)
    prior = ()
    for rounds in range(3):
        from_b = pair_up(to_b, CHIPS)
        from_a = pair_up(to_a, CORES) if rounds else over_both(to_a, lambda t, p: (t ^ 2, p ^ 1))
        if rounds == 0:
            *kept, w_in, steps = run_first(0, lat, from_a, *smalls, w_conv, w_mid, w_out)
        else:
            kept = run_first(rounds, lat, from_a, *prior, w_in, steps, w_mid, w_out)
        done = run_second(rounds, lat, from_b, *prior, *kept, w_in, w_mid, w_out, steps)
        if rounds < 2:
            *prior, to_a, to_b = done
    got = [done[0]]
    for k in (1, 2, 3):
        got.append(across(done[k], k))
    return join(got).reshape(2, C, ROWS, 448)


def solution(mesh):
    in_specs = (P(None, "pix", None), P("tm"), P("tm", None), P(), P(), P())
    out_specs = P("tm", None, "pix", None)
    return jax.shard_map(shards, mesh=mesh, in_specs=in_specs, out_specs=out_specs, check_vma=False)
```
